32 devices in a mesh: outer: 4 (over y, core), row: 4 (over z), col: 2 (over x).
Axes of the slice: x: 2, y: 2, z: 4, core: 2. Of those that a mesh axis runs over, the one named last changes fastest.
Arguments:
- activations: bfloat16 [2048, 9216], P(('outer', 'col'), 'row'), may hold values from -13 to 13
- out_grads: bfloat16 [2048, 8192], P(('outer', 'row'), 'col'), may hold values from -13 to 13
- row_moment: float32 [9216], P(('row', 'outer')), may hold values from 0.3 to 3
- col_moment: float32 [8192], P('col'), may hold values from 0.3 to 3
Outputs:
- update: bfloat16 [9216, 8192], P(('row', 'outer'), 'col')
- new_row: float32 [9216], P(('row', 'outer'))
- new_col: float32 [8192], P('col')
The draws below stay inside these ranges and needn't reach their ends.
All inputs are finite; a program needn't handle non-finite values.
Results may differ from the reference program's by a relative error of at most 0.001.
Values may be sent and summed in bfloat16 or wider, within the bound.
A program may use at most 128 MiB of HBM per device.

```python
import math
import jax
import jax.numpy as jnp
from jax import lax

D = 9216
F = 8192
STEP = 2
TOKENS = 2048


def scaled_block(key, count, width):
    first, second = jax.random.split(key)
    position = jnp.arange(width, dtype=jnp.float32) / max(width - 1, 1)
    rough = 10.0 ** jax.random.uniform(second, (width,), jnp.float32, -0.25, 0.25)
    base = jax.random.truncated_normal(first, -4.0, 4.0, (count, width), jnp.float32)
    rising = jnp.sqrt((1.0 + 2.0 * position) / 3.0) * 1.7320508
    return (base * (rough * rising)[None, :]).astype(jnp.bfloat16)


def draw_activations(key, part):
    return scaled_block(jax.random.fold_in(key, 11), TOKENS, D)


def draw_out_grads(key, part):
    return scaled_block(jax.random.fold_in(key, 23), TOKENS, F)


def block_scale(key, dims, pieces, least, high):
    def one(axis_at, shards_of):
        draws = jax.random.uniform(jax.random.fold_in(jax.random.fold_in(key, 6), axis_at), (shards_of,), jnp.float32, least / len(pieces), high / len(pieces))
        return jnp.repeat(jnp.exp(draws), dims[axis_at] // shards_of).reshape((-1,) + (1,) * (len(dims) - axis_at - 1))

    loudness = one(*pieces[0])
    for cut in pieces[1:]:
        loudness = loudness * one(*cut)
    return loudness


def setup_inputs(seed: int = 0) -> dict:
    arg_keys = jax.random.split(jax.random.key(seed), 5)
    activations = draw_activations(jax.random.fold_in(arg_keys[4], 71), 0)
    out_grads = draw_out_grads(jax.random.fold_in(arg_keys[4], 71), 0)
    row_moment = jnp.clip(jnp.exp(math.log(3.0) - 2.3025851 * jax.random.uniform(arg_keys[2], (D,), jnp.float32) ** block_scale(arg_keys[2], (D,), ((0, 16),), -0.2, 0.2)), 0.3, 3.0)
    col_moment = jnp.clip(jnp.exp(math.log(3.0) - 2.3025851 * jax.random.uniform(arg_keys[3], (F,), jnp.float32) ** block_scale(arg_keys[3], (F,), ((0, 2),), -0.2, 0.2)), 0.3, 3.0)
    return {"activations": activations, "out_grads": out_grads, "row_moment": row_moment, "col_moment": col_moment}


def reference(activations, out_grads, row_moment, col_moment):
    gradient = lax.dot_general(activations, out_grads, (((0,), (0,)), ((), ())), preferred_element_type=jnp.float32)
    gradient = gradient * (1.0 / TOKENS ** 0.5)
    squares = gradient * gradient
    row_squares = lax.optimization_barrier(jnp.sum(squares, axis=1))
    col_squares = lax.optimization_barrier(jnp.sum(squares, axis=0))
    decay_rate = 1.0 - STEP ** (-0.8)
    new_row = decay_rate * row_moment + (1.0 - decay_rate) * row_squares / F
    new_col = decay_rate * col_moment + (1.0 - decay_rate) * col_squares / D
    moment_total = jnp.sum(new_row)
    factor = lax.rsqrt(new_row[:, None] * new_col[None, :] * (D / moment_total))
    update = (gradient * factor).astype(jnp.bfloat16)
    return (update, new_row, new_col)
```

```python
import functools

import jax
import jax.numpy as jnp
from jax import lax
from jax.experimental import pallas as pl
from jax.experimental.pallas import tpu as pltpu
from jax.sharding import PartitionSpec as P

D = 9216
F = 8192
STEP = 2
MESH = pl.DeviceIdType.MESH


def cuts(width):
    unit = width // 128
    share, *edges = [round(unit * e / 32) * 128 for e in (7, 16, 24, 28, 32)]
    fine = [(a, b - a) for a, b in zip([0] + edges[:-1], edges)]
    chain = [[0], [1], [2, 3]]
    by_y = (0, share)
    by_z = [(share, edges[0] - share)] + fine[1:]
    return fine, chain, by_y, by_z


def each(first, last, f):
    if last - first <= 32:
        for k in range(first, last):
            f(k)
    else:
        pl.loop(first, last)(f)


def kernel(
    nout, nz, ncol, scale, decay,
    raw_ref, g_ref, rm_hbm, cm_hbm,
    acc, nr_ref, byrow_ref, nc_ref, bycol_ref,
    gs, av, raw, a_ref, rm_ref, cm_ref, rowp, early, earlyz, late, others, rowbuf,
    gz_recv, gy_recv, op_recv, od_recv, a1_recv, a2_recv,
    zp_send, zm_send, x_send, y_send, p_send, a1_send, a2_send, loc_sem,
    e_sem, ez_sem, l_sem, o_sem, r_sem, ready,
):
    tg, width = g_ref.shape
    rows, ta = av.shape[1], av.shape[2]
    fine, chain, by_y, by_z = cuts(width)
    last = len(fine) - 1
    wide = early.shape[2]
    o = lax.axis_index("outer")
    z = lax.axis_index("row")
    x = lax.axis_index("col")
    y, core = o // 2, o % 2
    oy = (1 - y) * 2 + core
    op = y * 2 + (1 - core)
    od = (1 - y) * 2 + (1 - core)
    mate = z + 1 - 2 * (z % 2)
    up = {"row": jnp.minimum(z + 1, nz - 1)}
    down = {"row": jnp.maximum(z - 1, 0)}

    def remote(src, dst, s, r, dev):
        return pltpu.make_async_remote_copy(
            src_ref=src, dst_ref=dst, send_sem=s, recv_sem=r, device_id=dev, device_id_type=MESH
        )

    def settle(ref, sem):
        pltpu.make_async_copy(ref, ref, sem).wait()

    load_a = pltpu.make_async_copy(raw_ref, raw, loc_sem.at[2])
    load_a.start()
    load_rm = pltpu.make_async_copy(rm_hbm, rm_ref, loc_sem.at[3])
    load_cm = pltpu.make_async_copy(cm_hbm, cm_ref, loc_sem.at[4])
    load_rm.start()
    load_cm.start()
    barrier = pltpu.get_barrier_semaphore()
    for d in range(1, nout):
        pl.semaphore_signal(barrier, inc=1, device_id={"outer": (o + d) % nout}, device_id_type=MESH)

    @pl.when(z > 0)
    def _():
        pl.semaphore_signal(barrier, inc=1, device_id=down, device_id_type=MESH)

    @pl.when(z < nz - 1)
    def _():
        pl.semaphore_signal(barrier, inc=1, device_id=up, device_id_type=MESH)

    for d in range(1, ncol):
        pl.semaphore_signal(barrier, inc=1, device_id={"col": (x + d) % ncol}, device_id_type=MESH)
    ends = jnp.where(z > 0, 1, 0) + jnp.where(z < nz - 1, 1, 0)
    pl.semaphore_wait(barrier, nout + ncol - 2 + ends)

    def slots(oo, zz, count, cols):
        start = pl.multiple_of((oo * nz + zz) * tg, tg)
        return gs.at[pl.ds(start, count * tg), pl.ds(*cols)]

    def place(oo, zz, cols):
        return slots(oo, zz, 1, cols)

    def merged(c):
        first, end = fine[chain[c][0]], fine[chain[c][-1]]
        return (first[0], end[0] + end[1] - first[0])

    full = (0, width)

    def to_up(src, zz, c):
        return remote(src, place(o, zz, merged(c)), zp_send, gz_recv.at[zz, c], up)

    def to_down(src, zz, c):
        return remote(src, place(o, zz, merged(c)), zm_send, gz_recv.at[zz, c], down)

    def to_y(src, zz, cols, j, sem):
        return remote(src, place(o, zz, cols), sem, gy_recv.at[zz, j], {"outer": oy})

    def near(src, zz, c):
        return remote(src, place(o, zz, merged(c)), p_send, op_recv.at[c], {"outer": op})

    def far(zz, cols, h):
        here = place(oy, zz, cols)
        return remote(here, here, p_send, od_recv.at[h], {"outer": op})

    for c in range(len(chain)):
        own = g_ref.at[:, pl.ds(*merged(c))]

        @pl.when(z < nz - 1)
        def _():
            to_up(own, z, c).start()

        @pl.when(z > 0)
        def _():
            to_down(own, z, c).start()

        if c == 0:
            to_y(g_ref, z, full, 0, y_send.at[0]).start()
        near(own, z, c).start()

    def a_first(d):
        target = (o + d) % nout
        return remote(a_ref.at[target], av.at[o * ncol + x], a1_send, a1_recv.at[o], {"outer": target})

    def a_second(oo, d, own=False):
        k = oo * ncol + x
        return remote(a_ref.at[o] if own else av.at[k], av.at[k], a2_send, a2_recv, {"col": (x + d) % ncol})

    local_g = pltpu.make_async_copy(g_ref, slots(o, z, 1, full), loc_sem.at[0])
    local_a = pltpu.make_async_copy(a_ref.at[o], av.at[o * ncol + x], loc_sem.at[1])
    local_g.start()
    load_a.wait()
    turned = jnp.transpose(raw[...])
    for k in range(nout):
        a_ref[k] = turned[k * rows : (k + 1) * rows]

    def pass_on(oo):
        k = oo * ncol + x
        remote(av.at[k], av.at[k], a1_send, a1_recv.at[oo], {"outer": oy}).wait_recv()
        for d in range(1, ncol):
            a_second(oo, d).start()

    def landed(zz, cols, j):
        here = place(oy, zz, cols)
        remote(here, here, y_send.at[0], gy_recv.at[zz, j], {"outer": oy}).wait_recv()

    def take(zz, h):
        landed(zz, fine[h], h)
        far(zz, fine[h], h).start()

    def take_mate(h):
        if h == 0:
            landed(mate, by_y, 0)
            far(mate, by_y, 0).start()
        landed(mate, by_z[h], h + 1)
        far(mate, by_z[h], h).start()

    def relay(zz, c, onward):
        here = place(o, zz, merged(c))
        remote(here, here, zp_send, gz_recv.at[zz, c], up).wait_recv()
        onward(here)

        @pl.when(zz != mate)
        def _():
            for j in chain[c]:
                to_y(place(o, zz, fine[j]), zz, fine[j], j, y_send.at[0]).start()

        if c == 0:
            @pl.when(zz == mate)
            def _():
                to_y(place(o, zz, by_y), zz, by_y, 0, y_send.at[1]).start()

        near(here, zz, c).start()

    def extra(act):
        for h in range(len(fine)):
            here = place(oy, z, by_z[h])

            @pl.when(mate > z)
            def _():
                act(remote(here, here, x_send, gy_recv.at[z, h + 1], up))

            @pl.when(mate < z)
            def _():
                act(remote(here, here, x_send, gy_recv.at[z, h + 1], down))

    def dots(oo, cols):
        total = None
        for k in range(ncol):
            block = oo * ncol + k
            part = jnp.dot(
                av[block],
                gs[pl.ds(pl.multiple_of(block * ta, ta), ta), cols],
                preferred_element_type=jnp.float32,
            )
            total = part if total is None else total + part
        return total

    def tiles(cols, f):
        start, size = cols
        tile = 512 if size % 512 == 0 else size

        @pl.loop(0, size // tile)
        def _(j):
            f(pl.multiple_of(j * tile, 128), tile)

    def first_half(c):
        slots_here = slots(op, 0, nz, merged(c))
        remote(slots_here, slots_here, p_send, op_recv.at[c], {"outer": op}).wait_recv()
        base = merged(c)[0]

        def one(offset, tile):
            cols = pl.ds(pl.multiple_of(base + offset, 128), tile)
            acc[:, cols] = dots(o, cols) + dots(op, cols)

        tiles(merged(c), one)

    for s in range(1, nz):
        if s == nz - 1:
            local_g.wait()
            local_a.wait()
            settle(av.at[pl.ds(0, (ncol - 1) * nout)], a2_recv)
        for c in range(len(chain)):
            @pl.when(z - s >= 0)
            def _():
                def onward(here):
                    @pl.when(z < nz - 1)
                    def _():
                        to_up(here, z - s, c).start()

                relay(z - s, c, onward)

            @pl.when(z + s < nz)
            def _():
                def onward(here):
                    @pl.when(z > 0)
                    def _():
                        to_down(here, z + s, c).start()

                relay(z + s, c, onward)

            if s == 1 and c == 0:
                for d in range(1, nout):
                    a_first(d).start()
                for d in range(1, ncol):
                    a_second(o, d, True).start()
                local_a.start()
            if s == nz - 1:
                first_half(c)

        if s == 1:
            landed(z, full, 0)
            for h in range(len(fine)):
                far(z, fine[h], h).start()
            pass_on(op)
        if s == min(2, nz - 1):
            for c in range(2):
                pass_on((1 - y) * 2 + c)
        if s == max(nz - 2, 1):
            extra(lambda c: c.start())
        if 1 < s < nz - 1:
            for zz in (z - (s - 1), z + (s - 1)):
                @pl.when((zz >= 0) & (zz < nz) & (zz != mate))
                def _():
                    for h in range(len(fine)):
                        take(zz, h)

    rowp[...] = jnp.zeros_like(rowp)
    load_rm.wait()
    load_cm.wait()
    old = rm_ref[...].reshape(1, rows)
    old_share = jnp.broadcast_to(jnp.sum(old, axis=1, keepdims=True) * (decay / ncol / 128), (1, 128))

    def finish(h, split=False):
        begin, size = fine[h]
        sums, shift = (early, 0) if begin < wide else (late, wide)

        def od_wait():
            here = slots(od, 0, nz, fine[h])
            remote(here, here, p_send, od_recv.at[h], {"outer": op}).wait_recv()

        def one(offset, tile):
            cols = pl.ds(pl.multiple_of(begin + offset, 128), tile)
            there = pl.ds(pl.multiple_of(begin - shift + offset, 128), tile)
            grad = (acc[:, cols] + dots(od, cols)) * scale if split else (acc[:, cols] + (dots(oy, cols) + dots(od, cols))) * scale
            acc[:, cols] = grad
            squares = grad * grad
            part = squares[:, :128]
            for i in range(1, tile // 128):
                part = part + squares[:, i * 128 : (i + 1) * 128]
            rowp[...] += part
            sums[0, :, there] = jnp.sum(squares, axis=0, keepdims=True)

        def ahead(offset, tile):
            cols = pl.ds(pl.multiple_of(begin + offset, 128), tile)
            acc[:, cols] = acc[:, cols] + dots(oy, cols)

        if split:
            tiles(fine[h], ahead)
        od_wait()
        tiles(fine[h], one)

    def e_first(d):
        return remote(early.at[0], early.at[nout - d], e_sem.at[0], e_sem.at[1], {"outer": (o + d) % nout})

    def e_second(d):
        return remote(earlyz.at[0], earlyz.at[nz - d], ez_sem.at[0], ez_sem.at[1], {"row": (z + d) % nz})

    for h in range(len(fine)):
        for s in range(nz - 2, nz):
            for zz in (z - s, z + s):
                @pl.when((zz >= 0) & (zz < nz) & (zz != mate))
                def _():
                    take(zz, h)

        take_mate(h)
        if h == last:
            settle(early.at[pl.ds(1, nout - 1)], e_sem.at[1])
            earlyz[0] = jnp.sum(early[...], axis=0)
            for d in range(1, nz):
                e_second(d).start()
        finish(h, h == last)
        if fine[h][0] + fine[h][1] == wide:
            for d in range(1, nout):
                e_first(d).start()
            for d in range(1, ncol):
                pl.semaphore_signal(ready, inc=1, device_id={"col": (x + d) % ncol}, device_id_type=MESH)

    group = nout * nz
    rest = width - wide

    def mirror(k):
        return ((nout - k // nz) % nout) * nz + (nz - k % nz) % nz

    def peer(k, c):
        return {"outer": (o + k // nz) % nout, "row": (z + k % nz) % nz, "col": (x + c) % ncol}

    def send_late(k):
        remote(late.at[0], late.at[mirror(k)], l_sem.at[0], l_sem.at[1], peer(k, 0)).start()

    late[0, :, pl.ds(rest, 128)] = jnp.sum(rowp[...], axis=0, keepdims=True) * ((1.0 - decay) / F) + old_share
    each(1, group, send_late)
    pl.semaphore_wait(ready, ncol - 1)
    for d in range(1, ncol):
        def send_other(k):
            slot = (ncol - d - 1) * group + mirror(k)
            remote(late.at[0, :, pl.ds(rest, 128)], others.at[slot], o_sem.at[0], o_sem.at[1], peer(k, d)).start()

        each(0, group, send_other)
    rowbuf[0] = jnp.sum(jnp.transpose(rowp[...]), axis=0, keepdims=True)

    def r_first(d):
        return remote(rowbuf.at[0], rowbuf.at[ncol - d], r_sem.at[0], r_sem.at[1], {"col": (x + d) % ncol})

    for d in range(1, ncol):
        r_first(d).start()
    settle(rowbuf.at[pl.ds(1, ncol - 1)], r_sem.at[1])
    row_sq = jnp.sum(rowbuf[...], axis=0)
    new_row = decay * old + (1.0 - decay) * row_sq / F
    nr_ref[...] = new_row
    byrow_ref[...] = jnp.transpose(jnp.broadcast_to(lax.rsqrt(new_row), (128, rows)))
    settle(earlyz.at[pl.ds(1, nz - 1)], ez_sem.at[1])
    cm = cm_ref[...].reshape(1, width)
    new_early = decay * cm[:, :wide] + (1.0 - decay) * jnp.sum(earlyz[...], axis=0) / D
    nc_ref[:, :wide] = new_early
    settle(late.at[pl.ds(1, group - 1)], l_sem.at[1])
    arrived = jnp.sum(late[...], axis=0)
    new_late = decay * cm[:, wide:] + (1.0 - decay) * arrived[:, :rest] / D
    nc_ref[:, wide:] = new_late
    settle(others, o_sem.at[1])
    total = jnp.sum(arrived[:, rest:] + jnp.sum(others[...], axis=0), axis=1, keepdims=True)
    factor = D / total
    bycol_ref[:, :wide] = lax.rsqrt(new_early * factor)
    bycol_ref[:, wide:] = lax.rsqrt(new_late * factor)

    for k in range(nz):
        if k < nz - 1:
            @pl.when(z == k)
            def _():
                settle(slots(0, 0, k + 1, full), zp_send)

        if k > 0:
            @pl.when(z == k)
            def _():
                settle(slots(0, 0, nz - k, full), zm_send)

    settle(slots(0, 0, nz - 1, full), y_send.at[0])
    settle(slots(0, 0, 1, by_y), y_send.at[1])
    settle(slots(0, 0, 2 * nz, full), p_send)
    settle(slots(0, 0, 1, (by_y[1], width - by_y[1])), x_send)
    settle(av.at[pl.ds(0, nout - 1)], a1_send)
    settle(av.at[pl.ds(0, (ncol - 1) * nout)], a2_send)
    settle(early.at[pl.ds(1, nout - 1)], e_sem.at[0])
    settle(earlyz.at[pl.ds(1, nz - 1)], ez_sem.at[0])
    settle(late.at[pl.ds(1, group - 1)], l_sem.at[0])
    settle(others, o_sem.at[0])
    settle(rowbuf.at[pl.ds(1, ncol - 1)], r_sem.at[0])


def update_kernel(step, grad_ref, byrow_ref, bycol_ref, nr_ref, nc_ref, out_hbm, row_hbm, col_hbm, out, row, col, sem):
    parts = out.shape[0] // step
    row[...] = nr_ref[...].reshape(row.shape)
    col[...] = nc_ref[...].reshape(col.shape)
    copies = [
        pltpu.make_async_copy(row, row_hbm, sem.at[parts]),
        pltpu.make_async_copy(col, col_hbm, sem.at[parts + 1]),
    ]
    for c in copies:
        c.start()
    for k in range(parts):
        here = pl.ds(k * step, step)
        out[here, :] = (grad_ref[here, :] * byrow_ref[here, :1] * bycol_ref[...]).astype(out.dtype)
        copies.append(pltpu.make_async_copy(out.at[here], out_hbm.at[here], sem.at[k]))
        copies[-1].start()
    for c in copies:
        c.wait()


def body(nout, nz, ncol, activations, out_grads, row_moment, col_moment):
    rows, width = row_moment.shape[0], col_moment.shape[0]
    ta, tg = activations.shape[0], out_grads.shape[0]
    tokens = ta * ncol * nout
    decay = 1.0 - STEP ** (-0.8)
    f32, bf16 = jnp.float32, jnp.bfloat16
    vmem = pl.BlockSpec(memory_space=pltpu.VMEM)
    hbm = pl.BlockSpec(memory_space=pl.ANY)
    dma = pltpu.SemaphoreType.DMA
    fine, chain, _, _ = cuts(width)
    wide = fine[1][0] + fine[1][1]
    grad, new_row, by_row, new_col, by_col = pl.pallas_call(
        functools.partial(kernel, nout, nz, ncol, 1.0 / tokens**0.5, decay),
        out_shape=(
            pltpu.VMEM((rows, width), f32),
            pltpu.VMEM((1, rows), f32),
            pltpu.VMEM((rows, 128), f32),
            pltpu.VMEM((1, width), f32),
            pltpu.VMEM((1, width), f32),
        ),
        in_specs=[hbm] * 4,
        out_specs=(vmem,) * 5,
        scratch_shapes=[
            pltpu.VMEM((tokens, width), bf16),
            pltpu.VMEM((nout * ncol, rows, ta), bf16),
            pltpu.VMEM(activations.shape, bf16),
            pltpu.VMEM((nout, rows, ta), bf16),
            pltpu.VMEM((rows,), f32),
            pltpu.VMEM((width,), f32),
            pltpu.VMEM((rows, 128), f32),
            pltpu.VMEM((nout, 1, wide), f32),
            pltpu.VMEM((nz, 1, wide), f32),
            pltpu.VMEM((nout * nz, 1, width - wide + 128), f32),
            pltpu.VMEM(((ncol - 1) * nout * nz, 1, 128), f32),
            pltpu.VMEM((ncol, 1, rows), f32),
            dma((nz, len(chain))),
            dma((nz, len(fine) + 1)),
            dma((len(chain),)),
            dma((len(fine),)),
            dma((nout,)),
            dma(()),
            dma(()),
            dma(()),
            dma(()),
            dma((2,)),
            dma(()),
            dma(()),
            dma(()),
            dma((5,)),
            dma((2,)), dma((2,)), dma((2,)), dma((2,)), dma((2,)),
            pltpu.SemaphoreType.REGULAR,
        ],
        compiler_params=pltpu.CompilerParams(
            collective_id=0, has_side_effects=True, vmem_limit_bytes=44 * 1024 * 1024
        ),
    )(
        activations,
        out_grads,
        pltpu.with_memory_space_constraint(row_moment, pltpu.HBM),
        pltpu.with_memory_space_constraint(col_moment, pltpu.HBM),
    )
    parts = next(n for n in (9, 6, 4, 3, 2, 1) if n == 1 or rows % (n * 16) == 0)
    return pl.pallas_call(
        functools.partial(update_kernel, rows // parts),
        out_shape=(
            jax.ShapeDtypeStruct((rows, width), bf16),
            jax.ShapeDtypeStruct((rows,), f32),
            jax.ShapeDtypeStruct((width,), f32),
        ),
        in_specs=[vmem] * 5,
        out_specs=(hbm,) * 3,
        scratch_shapes=[
            pltpu.VMEM((rows, width), bf16),
            pltpu.VMEM((rows,), f32),
            pltpu.VMEM((width,), f32),
            dma((parts + 2,)),
        ],
        compiler_params=pltpu.CompilerParams(vmem_limit_bytes=24 * 1024 * 1024),
    )(grad, by_row, by_col, new_row, new_col)


def solution(mesh):
    nout, nz, ncol = mesh.shape["outer"], mesh.shape["row"], mesh.shape["col"]
    return jax.shard_map(
        functools.partial(body, nout, nz, ncol),
        mesh=mesh,
        in_specs=(
            P(("outer", "col"), "row"),
            P(("outer", "row"), "col"),
            P(("row", "outer")),
            P("col"),
        ),
        out_specs=(P(("row", "outer"), "col"), P(("row", "outer")), P("col")),
        check_vma=False,
    )
```

```python
import functools

import jax
import jax.numpy as jnp
from jax import lax
from jax.experimental import pallas as pl
from jax.experimental.pallas import tpu as pltpu
from jax.sharding import PartitionSpec as P

D = 9216
F = 8192
STEP = 2
MESH = pl.DeviceIdType.MESH


def cuts(width):
    unit = width // 128
    edges = [round(unit * e / 32) * 128 for e in (8, 16, 24, 28, 32)]
    share = min(round(unit * 7 / 32) * 128, edges[0] - 128)
    fine = [(a, b - a) for a, b in zip([0] + edges[:-1], edges)]
    chain = [[0, 1], [2], [3, 4]]
    by_y = (0, share)
    by_z = [(share, edges[0] - share)] + fine[1:]
    return fine, chain, by_y, by_z


def each(first, last, f):
    if last - first <= 32:
        for k in range(first, last):
            f(k)
    else:
        pl.loop(first, last)(f)


def kernel(
    nout, nz, ncol, scale, decay,
    raw_ref, g_ref, rm_hbm, cm_hbm,
    acc, nr_ref, byrow_ref, nc_ref, bycol_ref,
    gs, av, raw, a_ref, rm_ref, cm_ref, rowp, early, earlyz, late, others, rowbuf,
    gz_recv, gy_recv, far_recv, mate_recv, op_recv, od_recv, a1_recv, a2_recv,
    zp_send, zm_send, x_send, y_send, p_send, a1_send, a2_send, loc_sem,
    e_sem, ez_sem, l_sem, o_sem, r_sem, ready,
):
    tg, width = g_ref.shape
    rows, ta = av.shape[1], av.shape[2]
    fine, chain, by_y, by_z = cuts(width)
    last = len(fine) - 1
    wide = early.shape[2]
    o = lax.axis_index("outer")
    z = lax.axis_index("row")
    x = lax.axis_index("col")
    y, core = o // 2, o % 2
    oy = (1 - y) * 2 + core
    op = y * 2 + (1 - core)
    od = (1 - y) * 2 + (1 - core)
    mate = z + 1 - 2 * (z % 2)
    end = jnp.where(z < nz // 2, nz - 1, 0)
    up = {"row": jnp.minimum(z + 1, nz - 1)}
    down = {"row": jnp.maximum(z - 1, 0)}

    def remote(src, dst, s, r, dev):
        return pltpu.make_async_remote_copy(
            src_ref=src, dst_ref=dst, send_sem=s, recv_sem=r, device_id=dev, device_id_type=MESH
        )

    def settle(ref, sem):
        pltpu.make_async_copy(ref, ref, sem).wait()

    load_a = pltpu.make_async_copy(raw_ref, raw, loc_sem.at[1])
    load_a.start()
    load_rm = pltpu.make_async_copy(rm_hbm, rm_ref, loc_sem.at[2])
    load_cm = pltpu.make_async_copy(cm_hbm, cm_ref, loc_sem.at[3])
    load_rm.start()
    load_cm.start()
    barrier = pltpu.get_barrier_semaphore()
    for d in range(1, nout):
        pl.semaphore_signal(barrier, inc=1, device_id={"outer": (o + d) % nout}, device_id_type=MESH)

    @pl.when(z > 0)
    def _():
        pl.semaphore_signal(barrier, inc=1, device_id=down, device_id_type=MESH)

    @pl.when(z < nz - 1)
    def _():
        pl.semaphore_signal(barrier, inc=1, device_id=up, device_id_type=MESH)

    for d in range(1, ncol):
        pl.semaphore_signal(barrier, inc=1, device_id={"col": (x + d) % ncol}, device_id_type=MESH)
    ends = jnp.where(z > 0, 1, 0) + jnp.where(z < nz - 1, 1, 0)
    pl.semaphore_wait(barrier, nout + ncol - 2 + ends)

    def slots(oo, zz, count, cols):
        start = pl.multiple_of((oo * nz + zz) * tg, tg)
        return gs.at[pl.ds(start, count * tg), pl.ds(*cols)]

    def place(oo, zz, cols):
        return slots(oo, zz, 1, cols)

    def merged(c):
        first, end = fine[chain[c][0]], fine[chain[c][-1]]
        return (first[0], end[0] + end[1] - first[0])

    full = (0, width)

    def from_z(zz, c, at):
        return gz_recv.at[(zz - at - 1 + 2 * nz) % nz, c]

    def to_up(src, zz, c):
        return remote(src, place(o, zz, merged(c)), zp_send, from_z(zz, c, z + 1), up)

    def to_down(src, zz, c):
        return remote(src, place(o, zz, merged(c)), zm_send, from_z(zz, c, z - 1), down)

    def to_y(src, zz, cols, sem, got):
        return remote(src, place(o, zz, cols), sem, got, {"outer": oy})

    def near(src, zz, c):
        return remote(src, place(o, zz, merged(c)), p_send, op_recv.at[c], {"outer": op})

    def over(zz, cols, h):
        here = place(oy, zz, cols)
        return remote(here, here, p_send, od_recv.at[h], {"outer": op})

    for c in range(len(chain)):
        own = g_ref.at[:, pl.ds(*merged(c))]

        @pl.when(z < nz - 1)
        def _():
            to_up(own, z, c).start()

        @pl.when(z > 0)
        def _():
            to_down(own, z, c).start()

        if c == 0:
            to_y(g_ref, z, full, y_send.at[0], gy_recv.at[z]).start()
        near(own, z, c).start()

    def a_first(d):
        target = (o + d) % nout
        return remote(a_ref.at[target], av.at[o * ncol + x], a1_send, a1_recv.at[d - 1], {"outer": target})

    def a_second(oo, d, own=False):
        k = oo * ncol + x
        return remote(a_ref.at[o] if own else av.at[k], av.at[k], a2_send, a2_recv, {"col": (x + d) % ncol})

    local_g = pltpu.make_async_copy(g_ref, slots(o, z, 1, full), loc_sem.at[0])
    local_a = pltpu.make_async_copy(a_ref.at[o], av.at[o * ncol + x], loc_sem.at[1])
    local_g.start()
    load_a.wait()
    turned = jnp.transpose(raw[...])
    for k in range(nout):
        a_ref[k] = turned[k * rows : (k + 1) * rows]

    def pass_on(oo):
        k = oo * ncol + x
        remote(av.at[k], av.at[k], a1_send, a1_recv.at[(o - oo + nout) % nout - 1], {"outer": oy}).wait_recv()
        for d in range(1, ncol):
            a_second(oo, d).start()

    def landed(zz, cols, sem):
        here = place(oy, zz, cols)
        remote(here, here, y_send.at[0], sem, {"outer": oy}).wait_recv()

    def take_whole(zz):
        landed(zz, full, gy_recv.at[zz])
        for h in range(len(fine)):
            over(zz, fine[h], h).start()

    def take(h):
        landed(end, fine[h], far_recv.at[h])
        over(end, fine[h], h).start()
        if h == 0:
            landed(mate, by_y, mate_recv.at[0])
            over(mate, by_y, 0).start()
        landed(mate, by_z[h], mate_recv.at[h + 1])
        over(mate, by_z[h], h).start()

    def relay(zz, c, onward):
        here = place(o, zz, merged(c))
        remote(here, here, zp_send, from_z(zz, c, z), up).wait_recv()
        onward(here)

        @pl.when((zz != mate) & (zz != end))
        def _():
            to_y(here, zz, merged(c), y_send.at[0], gy_recv.at[zz]).start()

        @pl.when(zz == end)
        def _():
            for j in chain[c]:
                to_y(place(o, zz, fine[j]), zz, fine[j], y_send.at[0], far_recv.at[j]).start()

        if c == 0:
            @pl.when(zz == mate)
            def _():
                to_y(place(o, zz, by_y), zz, by_y, y_send.at[1], mate_recv.at[0]).start()

        near(here, zz, c).start()

    def extra():
        for h in range(len(fine)):
            here = place(oy, z, by_z[h])

            @pl.when(mate > z)
            def _():
                remote(here, here, x_send, mate_recv.at[h + 1], up).start()

            @pl.when(mate < z)
            def _():
                remote(here, here, x_send, mate_recv.at[h + 1], down).start()

    def dots(oo, cols):
        total = None
        for k in range(ncol):
            block = oo * ncol + k
            part = jnp.dot(
                av[block],
                gs[pl.ds(pl.multiple_of(block * ta, ta), ta), cols],
                preferred_element_type=jnp.float32,
            )
            total = part if total is None else total + part
        return total

    def tiles(cols, f):
        start, size = cols
        tile = 512 if size % 512 == 0 else size

        @pl.loop(0, size // tile)
        def _(j):
            f(pl.multiple_of(j * tile, 128), tile)

    def first_half(c):
        slots_here = slots(op, 0, nz, merged(c))
        remote(slots_here, slots_here, p_send, op_recv.at[c], {"outer": op}).wait_recv()
        base = merged(c)[0]

        def one(offset, tile):
            cols = pl.ds(pl.multiple_of(base + offset, 128), tile)
            acc[:, cols] = dots(o, cols) + dots(op, cols)

        tiles(merged(c), one)

    def whole_from(d):
        for zz in (z - d, z + d):
            @pl.when((zz >= 0) & (zz < nz) & (zz != mate) & (zz != end))
            def _():
                take_whole(zz)

    for s in range(1, nz):
        if s == nz - 1:
            local_g.wait()
            local_a.wait()
            settle(av.at[pl.ds(0, (ncol - 1) * nout)], a2_recv)
        for c in range(len(chain)):
            @pl.when(z - s >= 0)
            def _():
                def onward(here):
                    @pl.when(z < nz - 1)
                    def _():
                        to_up(here, z - s, c).start()

                relay(z - s, c, onward)

            @pl.when(z + s < nz)
            def _():
                def onward(here):
                    @pl.when(z > 0)
                    def _():
                        to_down(here, z + s, c).start()

                relay(z + s, c, onward)

            if s == 1 and c == 0:
                for d in range(1, nout):
                    a_first(d).start()
                for d in range(1, ncol):
                    a_second(o, d, True).start()
                local_a.start()
            if s == nz - 1:
                first_half(c)
                if c == len(chain) - 2:
                    for d in (nz - 2, nz - 1):
                        whole_from(d)

        if s == 1:
            take_whole(z)
            pass_on(op)
        if s == min(2, nz - 1):
            for c in range(2):
                pass_on((1 - y) * 2 + c)
        if s == max(nz - 2, 1):
            extra()
        if 1 < s < nz - 1:
            whole_from(s - 1)

    rowp[...] = jnp.zeros_like(rowp)
    load_rm.wait()
    load_cm.wait()
    old = rm_ref[...].reshape(1, rows)
    old_share = jnp.broadcast_to(jnp.sum(old, axis=1, keepdims=True) * (decay / ncol / 128), (1, 128))

    def finish(h, split=False):
        begin, size = fine[h]
        sums, shift = (early, 0) if begin < wide else (late, wide)

        def od_wait():
            here = slots(od, 0, nz, fine[h])
            remote(here, here, p_send, od_recv.at[h], {"outer": op}).wait_recv()

        def one(offset, tile):
            cols = pl.ds(pl.multiple_of(begin + offset, 128), tile)
            there = pl.ds(pl.multiple_of(begin - shift + offset, 128), tile)
            grad = (acc[:, cols] + dots(od, cols)) * scale if split else (acc[:, cols] + (dots(oy, cols) + dots(od, cols))) * scale
            acc[:, cols] = grad
            squares = grad * grad
            part = squares[:, :128]
            for i in range(1, tile // 128):
                part = part + squares[:, i * 128 : (i + 1) * 128]
            rowp[...] += part
            sums[0, :, there] = jnp.sum(squares, axis=0, keepdims=True)

        def ahead(offset, tile):
            cols = pl.ds(pl.multiple_of(begin + offset, 128), tile)
            acc[:, cols] = acc[:, cols] + dots(oy, cols)

        if split:
            tiles(fine[h], ahead)
        od_wait()
        tiles(fine[h], one)

    def e_first(d):
        return remote(early.at[0], early.at[nout - d], e_sem.at[0], e_sem.at[1], {"outer": (o + d) % nout})

    def e_second(d):
        return remote(earlyz.at[0], earlyz.at[nz - d], ez_sem.at[0], ez_sem.at[1], {"row": (z + d) % nz})

    for h in range(len(fine)):
        take(h)
        finish(h, h == last)
        if fine[h][0] + fine[h][1] == wide:
            for d in range(1, nout):
                e_first(d).start()
            for d in range(1, ncol):
                pl.semaphore_signal(ready, inc=1, device_id={"col": (x + d) % ncol}, device_id_type=MESH)

    group = nout * nz
    rest = width - wide

    def mirror(k):
        return ((nout - k // nz) % nout) * nz + (nz - k % nz) % nz

    def peer(k, c):
        return {"outer": (o + k // nz) % nout, "row": (z + k % nz) % nz, "col": (x + c) % ncol}

    def send_late(k):
        remote(late.at[0], late.at[mirror(k)], l_sem.at[0], l_sem.at[1], peer(k, 0)).start()

    late[0, :, pl.ds(rest, 128)] = jnp.sum(rowp[...], axis=0, keepdims=True) * ((1.0 - decay) / F) + old_share
    pl.semaphore_wait(ready, ncol - 1)
    for d in range(1, ncol):
        def send_other(k):
            slot = (ncol - d - 1) * group + mirror(k)
            remote(late.at[0, :, pl.ds(rest, 128)], others.at[slot], o_sem.at[0], o_sem.at[1], peer(k, d)).start()

        each(0, group, send_other)
    each(1, group, send_late)
    settle(early.at[pl.ds(1, nout - 1)], e_sem.at[1])
    earlyz[0] = jnp.sum(early[...], axis=0)
    for d in range(1, nz):
        e_second(d).start()
    rowbuf[0] = jnp.sum(jnp.transpose(rowp[...]), axis=0, keepdims=True)

    def r_first(d):
        return remote(rowbuf.at[0], rowbuf.at[ncol - d], r_sem.at[0], r_sem.at[1], {"col": (x + d) % ncol})

    for d in range(1, ncol):
        r_first(d).start()
    settle(rowbuf.at[pl.ds(1, ncol - 1)], r_sem.at[1])
    row_sq = jnp.sum(rowbuf[...], axis=0)
    new_row = decay * old + (1.0 - decay) * row_sq / F
    nr_ref[...] = new_row
    byrow_ref[...] = jnp.transpose(jnp.broadcast_to(lax.rsqrt(new_row), (128, rows)))
    settle(earlyz.at[pl.ds(1, nz - 1)], ez_sem.at[1])
    cm = cm_ref[...].reshape(1, width)
    new_early = decay * cm[:, :wide] + (1.0 - decay) * jnp.sum(earlyz[...], axis=0) / D
    nc_ref[:, :wide] = new_early
    settle(late.at[pl.ds(1, group - 1)], l_sem.at[1])
    arrived = jnp.sum(late[...], axis=0)
    new_late = decay * cm[:, wide:] + (1.0 - decay) * arrived[:, :rest] / D
    nc_ref[:, wide:] = new_late
    settle(others, o_sem.at[1])
    total = jnp.sum(arrived[:, rest:] + jnp.sum(others[...], axis=0), axis=1, keepdims=True)
    factor = D / total
    bycol_ref[:, :wide] = lax.rsqrt(new_early * factor)
    bycol_ref[:, wide:] = lax.rsqrt(new_late * factor)

    for k in range(nz):
        if k < nz - 1:
            @pl.when(z == k)
            def _():
                settle(slots(0, 0, k + 1, full), zp_send)

        if k > 0:
            @pl.when(z == k)
            def _():
                settle(slots(0, 0, nz - k, full), zm_send)

    settle(slots(0, 0, nz - 1, full), y_send.at[0])
    settle(slots(0, 0, 1, by_y), y_send.at[1])
    settle(slots(0, 0, 2 * nz, full), p_send)
    settle(slots(0, 0, 1, (by_y[1], width - by_y[1])), x_send)
    settle(av.at[pl.ds(0, nout - 1)], a1_send)
    settle(av.at[pl.ds(0, (ncol - 1) * nout)], a2_send)
    settle(early.at[pl.ds(1, nout - 1)], e_sem.at[0])
    settle(earlyz.at[pl.ds(1, nz - 1)], ez_sem.at[0])
    settle(late.at[pl.ds(1, group - 1)], l_sem.at[0])
    settle(others, o_sem.at[0])
    settle(rowbuf.at[pl.ds(1, ncol - 1)], r_sem.at[0])


def update_kernel(step, grad_ref, byrow_ref, bycol_ref, nr_ref, nc_ref, out_hbm, row_hbm, col_hbm, out, row, col, sem):
    parts = out.shape[0] // step
    row[...] = nr_ref[...].reshape(row.shape)
    col[...] = nc_ref[...].reshape(col.shape)
    copies = [
        pltpu.make_async_copy(row, row_hbm, sem.at[parts]),
        pltpu.make_async_copy(col, col_hbm, sem.at[parts + 1]),
    ]
    for c in copies:
        c.start()
    for k in range(parts):
        here = pl.ds(k * step, step)
        out[here, :] = (grad_ref[here, :] * jnp.tile(byrow_ref[here, :], (1, out.shape[1] // 128)) * bycol_ref[...]).astype(out.dtype)
        copies.append(pltpu.make_async_copy(out.at[here], out_hbm.at[here], sem.at[k]))
        copies[-1].start()
    for c in copies:
        c.wait()


def body(nout, nz, ncol, activations, out_grads, row_moment, col_moment):
    rows, width = row_moment.shape[0], col_moment.shape[0]
    ta, tg = activations.shape[0], out_grads.shape[0]
    tokens = ta * ncol * nout
    decay = 1.0 - STEP ** (-0.8)
    f32, bf16 = jnp.float32, jnp.bfloat16
    vmem = pl.BlockSpec(memory_space=pltpu.VMEM)
    hbm = pl.BlockSpec(memory_space=pl.ANY)
    dma = pltpu.SemaphoreType.DMA
    fine, chain, _, _ = cuts(width)
    wide = fine[2][0] + fine[2][1]
    grad, new_row, by_row, new_col, by_col = pl.pallas_call(
        functools.partial(kernel, nout, nz, ncol, 1.0 / tokens**0.5, decay),
        out_shape=(
            pltpu.VMEM((rows, width), f32),
            pltpu.VMEM((1, rows), f32),
            pltpu.VMEM((rows, 128), f32),
            pltpu.VMEM((1, width), f32),
            pltpu.VMEM((1, width), f32),
        ),
        in_specs=[hbm] * 4,
        out_specs=(vmem,) * 5,
        scratch_shapes=[
            pltpu.VMEM((tokens, width), bf16),
            pltpu.VMEM((nout * ncol, rows, ta), bf16),
            pltpu.VMEM(activations.shape, bf16),
            pltpu.VMEM((nout, rows, ta), bf16),
            pltpu.VMEM((rows,), f32),
            pltpu.VMEM((width,), f32),
            pltpu.VMEM((rows, 128), f32),
            pltpu.VMEM((nout, 1, wide), f32),
            pltpu.VMEM((nz, 1, wide), f32),
            pltpu.VMEM((nout * nz, 1, width - wide + 128), f32),
            pltpu.VMEM(((ncol - 1) * nout * nz, 1, 128), f32),
            pltpu.VMEM((ncol, 1, rows), f32),
            dma((nz - 1, len(chain))),
            dma((nz,)),
            dma((len(fine),)),
            dma((len(fine) + 1,)),
            dma((len(chain),)),
            dma((len(fine),)),
            dma((nout - 1,)),
            dma(()),
            dma(()),
            dma(()),
            dma(()),
            dma((2,)),
            dma(()),
            dma(()),
            dma(()),
            dma((4,)),
            dma((2,)), dma((2,)), dma((2,)), dma((2,)), dma((2,)),
            pltpu.SemaphoreType.REGULAR,
        ],
        compiler_params=pltpu.CompilerParams(
            collective_id=0, has_side_effects=True, vmem_limit_bytes=44 * 1024 * 1024
        ),
    )(
        activations,
        out_grads,
        pltpu.with_memory_space_constraint(row_moment, pltpu.HBM),
        pltpu.with_memory_space_constraint(col_moment, pltpu.HBM),
    )
    parts = next(n for n in (9, 6, 4, 3, 2, 1) if n == 1 or rows % (n * 16) == 0)
    return pl.pallas_call(
        functools.partial(update_kernel, rows // parts),
        out_shape=(
            jax.ShapeDtypeStruct((rows, width), bf16),
            jax.ShapeDtypeStruct((rows,), f32),
            jax.ShapeDtypeStruct((width,), f32),
        ),
        in_specs=[vmem] * 5,
        out_specs=(hbm,) * 3,
        scratch_shapes=[
            pltpu.VMEM((rows, width), bf16),
            pltpu.VMEM((rows,), f32),
            pltpu.VMEM((width,), f32),
            dma((parts + 2,)),
        ],
        compiler_params=pltpu.CompilerParams(vmem_limit_bytes=24 * 1024 * 1024),
    )(grad, by_row, by_col, new_row, new_col)


def solution(mesh):
    nout, nz, ncol = mesh.shape["outer"], mesh.shape["row"], mesh.shape["col"]
    return jax.shard_map(
        functools.partial(body, nout, nz, ncol),
        mesh=mesh,
        in_specs=(
            P(("outer", "col"), "row"),
            P(("outer", "row"), "col"),
            P(("row", "outer")),
            P("col"),
        ),
        out_specs=(P(("row", "outer"), "col"), P(("row", "outer")), P("col")),
        check_vma=False,
    )
```

```python
import functools

import jax
import jax.numpy as jnp
from jax import lax
from jax.experimental import pallas as pl
from jax.experimental.pallas import tpu as pltpu
from jax.sharding import PartitionSpec as P

D = 9216
F = 8192
STEP = 2
MESH = pl.DeviceIdType.MESH


def cuts(width):
    unit = width // 128
    edges = [round(unit * e / 32) * 128 for e in (8, 16, 24, 28, 32)]
    share = min(round(unit * 7 / 32) * 128, edges[0] - 128)
    fine = [(a, b - a) for a, b in zip([0] + edges[:-1], edges)]
    chain = [[0, 1], [2], [3, 4]]
    by_y = (0, share)
    by_z = [(share, edges[0] - share)] + fine[1:]
    return fine, chain, by_y, by_z


def each(first, last, f):
    if last - first <= 32:
        for k in range(first, last):
            f(k)
    else:
        pl.loop(first, last)(f)


def kernel(
    nout, nz, ncol, scale, decay,
    raw_ref, g_ref, rm_hbm, cm_hbm,
    acc, nr_ref, byrow_ref, nc_ref, bycol_ref,
    gs, av, raw, a_ref, rm_ref, cm_ref, rowp, early, earlyz, late, others, rowbuf,
    gz_recv, gy_recv, far_recv, mate_recv, op_recv, od_recv, a1_recv, a2_recv,
    g_send, p_send, a_send, loc_sem,
    e_sem, ez_sem, l_sem, o_sem, r_sem, ready,
):
    tg, width = g_ref.shape
    rows, ta = av.shape[1], av.shape[2]
    fine, chain, by_y, by_z = cuts(width)
    last = len(fine) - 1
    wide = early.shape[2]
    o = lax.axis_index("outer")
    z = lax.axis_index("row")
    x = lax.axis_index("col")
    y, core = o // 2, o % 2
    oy = (1 - y) * 2 + core
    op = y * 2 + (1 - core)
    od = (1 - y) * 2 + (1 - core)
    mate = z + 1 - 2 * (z % 2)
    end = jnp.where(z < nz // 2, nz - 1, 0)
    up = {"row": jnp.minimum(z + 1, nz - 1)}
    down = {"row": jnp.maximum(z - 1, 0)}

    def remote(src, dst, s, r, dev):
        return pltpu.make_async_remote_copy(
            src_ref=src, dst_ref=dst, send_sem=s, recv_sem=r, device_id=dev, device_id_type=MESH
        )

    def settle(ref, sem):
        pltpu.make_async_copy(ref, ref, sem).wait()

    load_a = pltpu.make_async_copy(raw_ref, raw, loc_sem.at[1])
    load_a.start()
    load_rm = pltpu.make_async_copy(rm_hbm, rm_ref, loc_sem.at[2])
    load_cm = pltpu.make_async_copy(cm_hbm, cm_ref, loc_sem.at[3])
    load_rm.start()
    load_cm.start()
    barrier = pltpu.get_barrier_semaphore()
    for d in range(1, nout):
        pl.semaphore_signal(barrier, inc=1, device_id={"outer": (o + d) % nout}, device_id_type=MESH)

    @pl.when(z > 0)
    def _():
        pl.semaphore_signal(barrier, inc=1, device_id=down, device_id_type=MESH)

    @pl.when(z < nz - 1)
    def _():
        pl.semaphore_signal(barrier, inc=1, device_id=up, device_id_type=MESH)

    for d in range(1, ncol):
        pl.semaphore_signal(barrier, inc=1, device_id={"col": (x + d) % ncol}, device_id_type=MESH)
    ends = jnp.where(z > 0, 1, 0) + jnp.where(z < nz - 1, 1, 0)
    pl.semaphore_wait(barrier, nout + ncol - 2 + ends)

    def slots(oo, zz, count, cols):
        start = pl.multiple_of((oo * nz + zz) * tg, tg)
        return gs.at[pl.ds(start, count * tg), pl.ds(*cols)]

    def place(oo, zz, cols):
        return slots(oo, zz, 1, cols)

    def merged(c):
        first, end = fine[chain[c][0]], fine[chain[c][-1]]
        return (first[0], end[0] + end[1] - first[0])

    full = (0, width)

    def from_z(zz, c, at):
        return gz_recv.at[(zz - at - 1 + 2 * nz) % nz, c]

    def to_up(src, zz, c):
        return remote(src, place(o, zz, merged(c)), g_send, from_z(zz, c, z + 1), up)

    def to_down(src, zz, c):
        return remote(src, place(o, zz, merged(c)), g_send, from_z(zz, c, z - 1), down)

    def to_y(src, zz, cols, sem, got):
        return remote(src, place(o, zz, cols), sem, got, {"outer": oy})

    def near(src, zz, c):
        return remote(src, place(o, zz, merged(c)), p_send, op_recv.at[c], {"outer": op})

    def over(zz, cols, h):
        here = place(oy, zz, cols)
        return remote(here, here, p_send, od_recv.at[h], {"outer": op})

    for c in range(len(chain)):
        own = g_ref.at[:, pl.ds(*merged(c))]

        @pl.when(z < nz - 1)
        def _():
            to_up(own, z, c).start()

        @pl.when(z > 0)
        def _():
            to_down(own, z, c).start()

        if c == 0:
            to_y(g_ref, z, full, g_send, gy_recv.at[z]).start()
        near(own, z, c).start()

    def a_first(d):
        target = (o + d) % nout
        return remote(a_ref.at[target], av.at[o * ncol + x], a_send, a1_recv.at[d - 1], {"outer": target})

    def a_second(oo, d, own=False):
        k = oo * ncol + x
        return remote(a_ref.at[o] if own else av.at[k], av.at[k], a_send, a2_recv, {"col": (x + d) % ncol})

    local_g = pltpu.make_async_copy(g_ref, slots(o, z, 1, full), loc_sem.at[0])
    local_a = pltpu.make_async_copy(a_ref.at[o], av.at[o * ncol + x], loc_sem.at[1])
    local_g.start()
    load_a.wait()
    turned = jnp.transpose(raw[...])
    for k in range(nout):
        a_ref[k] = turned[k * rows : (k + 1) * rows]

    def pass_on(oo):
        k = oo * ncol + x
        remote(av.at[k], av.at[k], a_send, a1_recv.at[(o - oo + nout) % nout - 1], {"outer": oy}).wait_recv()
        for d in range(1, ncol):
            a_second(oo, d).start()

    def landed(zz, cols, sem):
        here = place(oy, zz, cols)
        remote(here, here, g_send, sem, {"outer": oy}).wait_recv()

    def take_whole(zz):
        landed(zz, full, gy_recv.at[zz])
        for h in range(len(fine)):
            over(zz, fine[h], h).start()

    def take(h):
        landed(end, fine[h], far_recv.at[h])
        over(end, fine[h], h).start()
        landed(mate, fine[h], mate_recv.at[h])
        over(mate, fine[h], h).start()

    def relay(zz, c, onward):
        here = place(o, zz, merged(c))
        remote(here, here, g_send, from_z(zz, c, z), up).wait_recv()
        onward(here)

        @pl.when((zz != mate) & (zz != end))
        def _():
            to_y(here, zz, merged(c), g_send, gy_recv.at[zz]).start()

        @pl.when(zz == end)
        def _():
            for j in chain[c]:
                to_y(place(o, zz, fine[j]), zz, fine[j], g_send, far_recv.at[j]).start()

        if c == 0:
            @pl.when(zz == mate)
            def _():
                to_y(place(o, zz, by_y), zz, by_y, g_send, mate_recv.at[0]).start()

        near(here, zz, c).start()

    def extra():
        for h in range(len(fine)):
            here = place(oy, z, by_z[h])

            @pl.when(mate > z)
            def _():
                remote(here, here, g_send, mate_recv.at[h], up).start()

            @pl.when(mate < z)
            def _():
                remote(here, here, g_send, mate_recv.at[h], down).start()

    def dots(oo, cols):
        total = None
        for k in range(ncol):
            block = oo * ncol + k
            part = jnp.dot(
                av[block],
                gs[pl.ds(pl.multiple_of(block * ta, ta), ta), cols],
                preferred_element_type=jnp.float32,
            )
            total = part if total is None else total + part
        return total

    def tiles(cols, f):
        start, size = cols
        tile = 512 if size % 512 == 0 else size

        @pl.loop(0, size // tile)
        def _(j):
            f(pl.multiple_of(j * tile, 128), tile)

    def first_half(c):
        slots_here = slots(op, 0, nz, merged(c))
        remote(slots_here, slots_here, p_send, op_recv.at[c], {"outer": op}).wait_recv()
        base = merged(c)[0]

        def one(offset, tile):
            cols = pl.ds(pl.multiple_of(base + offset, 128), tile)
            acc[:, cols] = dots(o, cols) + dots(op, cols)

        tiles(merged(c), one)

    def whole_from(d):
        for zz in (z - d, z + d):
            @pl.when((zz >= 0) & (zz < nz) & (zz != mate) & (zz != end))
            def _():
                take_whole(zz)

    for s in range(1, nz):
        if s == nz - 1:
            local_g.wait()
            local_a.wait()
            settle(av.at[pl.ds(0, (ncol - 1) * nout)], a2_recv)
        for c in range(len(chain)):
            @pl.when(z - s >= 0)
            def _():
                def onward(here):
                    @pl.when(z < nz - 1)
                    def _():
                        to_up(here, z - s, c).start()

                relay(z - s, c, onward)

            @pl.when(z + s < nz)
            def _():
                def onward(here):
                    @pl.when(z > 0)
                    def _():
                        to_down(here, z + s, c).start()

                relay(z + s, c, onward)

            if s == 1 and c == 0:
                for d in range(1, nout):
                    a_first(d).start()
                for d in range(1, ncol):
                    a_second(o, d, True).start()
                local_a.start()
            if s == nz - 1:
                first_half(c)
                if c == len(chain) - 2:
                    for d in (nz - 2, nz - 1):
                        whole_from(d)

        if s == 1:
            take_whole(z)
            pass_on(op)
        if s == min(2, nz - 1):
            for c in range(2):
                pass_on((1 - y) * 2 + c)
        if s == max(nz - 2, 1):
            extra()
        if 1 < s < nz - 1:
            whole_from(s - 1)

    rowp[...] = jnp.zeros_like(rowp)
    load_rm.wait()
    load_cm.wait()
    old = rm_ref[...].reshape(1, rows)
    old_share = jnp.broadcast_to(jnp.sum(old, axis=1, keepdims=True) * (decay / ncol / 128), (1, 128))

    def finish(h, split=False):
        begin, size = fine[h]
        sums, shift = (early, 0) if begin < wide else (late, wide)

        def od_wait():
            here = slots(od, 0, nz, fine[h])
            remote(here, here, p_send, od_recv.at[h], {"outer": op}).wait_recv()

        def one(offset, tile):
            cols = pl.ds(pl.multiple_of(begin + offset, 128), tile)
            there = pl.ds(pl.multiple_of(begin - shift + offset, 128), tile)
            grad = (acc[:, cols] + dots(od, cols)) * scale if split else (acc[:, cols] + (dots(oy, cols) + dots(od, cols))) * scale
            acc[:, cols] = grad
            squares = grad * grad
            part = squares[:, :128]
            for i in range(1, tile // 128):
                part = part + squares[:, i * 128 : (i + 1) * 128]
            rowp[...] += part
            sums[0, :, there] = jnp.sum(squares, axis=0, keepdims=True)

        def ahead(offset, tile):
            cols = pl.ds(pl.multiple_of(begin + offset, 128), tile)
            acc[:, cols] = acc[:, cols] + dots(oy, cols)

        if split:
            tiles(fine[h], ahead)
        od_wait()
        tiles(fine[h], one)

    def e_first(d):
        return remote(early.at[0], early.at[nout - d], e_sem.at[0], e_sem.at[1], {"outer": (o + d) % nout})

    def e_second(d):
        return remote(earlyz.at[0], earlyz.at[nz - d], ez_sem.at[0], ez_sem.at[1], {"row": (z + d) % nz})

    @pl.when(core == 1)
    def _():
        take(0)

    for h in range(len(fine)):
        @pl.when(core == 0)
        def _():
            take(h)

        if h < last:
            @pl.when(core == 1)
            def _():
                take(h + 1)

        finish(h, h == last)
        if fine[h][0] + fine[h][1] == wide:
            for d in range(1, nout):
                e_first(d).start()
            for d in range(1, ncol):
                pl.semaphore_signal(ready, inc=1, device_id={"col": (x + d) % ncol}, device_id_type=MESH)

    group = nout * nz
    rest = width - wide

    def mirror(k):
        return ((nout - k // nz) % nout) * nz + (nz - k % nz) % nz

    def peer(k, c):
        return {"outer": (o + k // nz) % nout, "row": (z + k % nz) % nz, "col": (x + c) % ncol}

    def send_late(k):
        remote(late.at[0], late.at[mirror(k)], l_sem.at[0], l_sem.at[1], peer(k, 0)).start()

    late[0, :, pl.ds(rest, 128)] = jnp.sum(rowp[...], axis=0, keepdims=True) * ((1.0 - decay) / F) + old_share
    pl.semaphore_wait(ready, ncol - 1)
    for d in range(1, ncol):
        def send_other(k):
            slot = (ncol - d - 1) * group + mirror(k)
            remote(late.at[0, :, pl.ds(rest, 128)], others.at[slot], o_sem.at[0], o_sem.at[1], peer(k, d)).start()

        each(0, group, send_other)
    each(1, group, send_late)
    settle(early.at[pl.ds(1, nout - 1)], e_sem.at[1])
    earlyz[0] = jnp.sum(early[...], axis=0)
    for d in range(1, nz):
        e_second(d).start()
    rowbuf[0] = jnp.sum(jnp.transpose(rowp[...]), axis=0, keepdims=True)

    def r_first(d):
        return remote(rowbuf.at[0], rowbuf.at[ncol - d], r_sem.at[0], r_sem.at[1], {"col": (x + d) % ncol})

    for d in range(1, ncol):
        r_first(d).start()
    settle(rowbuf.at[pl.ds(1, ncol - 1)], r_sem.at[1])
    row_sq = jnp.sum(rowbuf[...], axis=0)
    new_row = decay * old + (1.0 - decay) * row_sq / F
    nr_ref[...] = new_row
    byrow_ref[...] = jnp.transpose(jnp.broadcast_to(lax.rsqrt(new_row), (128, rows)))
    settle(earlyz.at[pl.ds(1, nz - 1)], ez_sem.at[1])
    cm = cm_ref[...].reshape(1, width)
    new_early = decay * cm[:, :wide] + (1.0 - decay) * jnp.sum(earlyz[...], axis=0) / D
    nc_ref[:, :wide] = new_early
    settle(late.at[pl.ds(1, group - 1)], l_sem.at[1])
    arrived = jnp.sum(late[...], axis=0)
    new_late = decay * cm[:, wide:] + (1.0 - decay) * arrived[:, :rest] / D
    nc_ref[:, wide:] = new_late
    settle(others, o_sem.at[1])
    total = jnp.sum(arrived[:, rest:] + jnp.sum(others[...], axis=0), axis=1, keepdims=True)
    factor = D / total
    bycol_ref[:, :wide] = lax.rsqrt(new_early * factor)
    bycol_ref[:, wide:] = lax.rsqrt(new_late * factor)

    at_end = (z == 0) | (z == nz - 1)

    @pl.when(at_end)
    def _():
        settle(slots(0, 0, nz + 1, full), g_send)

    @pl.when(jnp.logical_not(at_end))
    def _():
        settle(slots(0, 0, 2 * nz + 1, full), g_send)

    settle(slots(0, 0, 2 * nz, full), p_send)
    settle(av.at[pl.ds(0, ncol * nout - 1)], a_send)
    settle(early.at[pl.ds(1, nout - 1)], e_sem.at[0])
    settle(earlyz.at[pl.ds(1, nz - 1)], ez_sem.at[0])
    settle(late.at[pl.ds(1, group - 1)], l_sem.at[0])
    settle(others, o_sem.at[0])
    settle(rowbuf.at[pl.ds(1, ncol - 1)], r_sem.at[0])


def update_kernel(step, grad_ref, byrow_ref, bycol_ref, nr_ref, nc_ref, out_hbm, row_hbm, col_hbm, out, row, col, sem):
    parts = out.shape[0] // step
    row[...] = nr_ref[...].reshape(row.shape)
    col[...] = nc_ref[...].reshape(col.shape)
    copies = [
        pltpu.make_async_copy(row, row_hbm, sem.at[parts]),
        pltpu.make_async_copy(col, col_hbm, sem.at[parts + 1]),
    ]
    for c in copies:
        c.start()
    for k in range(parts):
        here = pl.ds(k * step, step)
        out[here, :] = (grad_ref[here, :] * jnp.tile(byrow_ref[here, :], (1, out.shape[1] // 128)) * bycol_ref[...]).astype(out.dtype)
        copies.append(pltpu.make_async_copy(out.at[here], out_hbm.at[here], sem.at[k]))
        copies[-1].start()
    for c in copies:
        c.wait()


def body(nout, nz, ncol, activations, out_grads, row_moment, col_moment):
    rows, width = row_moment.shape[0], col_moment.shape[0]
    ta, tg = activations.shape[0], out_grads.shape[0]
    tokens = ta * ncol * nout
    decay = 1.0 - STEP ** (-0.8)
    f32, bf16 = jnp.float32, jnp.bfloat16
    vmem = pl.BlockSpec(memory_space=pltpu.VMEM)
    hbm = pl.BlockSpec(memory_space=pl.ANY)
    dma = pltpu.SemaphoreType.DMA
    fine, chain, _, _ = cuts(width)
    wide = fine[2][0] + fine[2][1]
    grad, new_row, by_row, new_col, by_col = pl.pallas_call(
        functools.partial(kernel, nout, nz, ncol, 1.0 / tokens**0.5, decay),
        out_shape=(
            pltpu.VMEM((rows, width), f32),
            pltpu.VMEM((1, rows), f32),
            pltpu.VMEM((rows, 128), f32),
            pltpu.VMEM((1, width), f32),
            pltpu.VMEM((1, width), f32),
        ),
        in_specs=[hbm] * 4,
        out_specs=(vmem,) * 5,
        scratch_shapes=[
            pltpu.VMEM((tokens, width), bf16),
            pltpu.VMEM((nout * ncol, rows, ta), bf16),
            pltpu.VMEM(activations.shape, bf16),
            pltpu.VMEM((nout, rows, ta), bf16),
            pltpu.VMEM((rows,), f32),
            pltpu.VMEM((width,), f32),
            pltpu.VMEM((rows, 128), f32),
            pltpu.VMEM((nout, 1, wide), f32),
            pltpu.VMEM((nz, 1, wide), f32),
            pltpu.VMEM((nout * nz, 1, width - wide + 128), f32),
            pltpu.VMEM(((ncol - 1) * nout * nz, 1, 128), f32),
            pltpu.VMEM((ncol, 1, rows), f32),
            dma((nz - 1, len(chain))),
            dma((nz,)),
            dma((len(fine),)),
            dma((len(fine),)),
            dma((len(chain),)),
            dma((len(fine),)),
            dma((nout - 1,)),
            dma(()),
            dma(()),
            dma(()),
            dma(()),
            dma((4,)),
            dma((2,)), dma((2,)), dma((2,)), dma((2,)), dma((2,)),
            pltpu.SemaphoreType.REGULAR,
        ],
        compiler_params=pltpu.CompilerParams(
            collective_id=0, has_side_effects=True, vmem_limit_bytes=44 * 1024 * 1024
        ),
    )(
        activations,
        out_grads,
        pltpu.with_memory_space_constraint(row_moment, pltpu.HBM),
        pltpu.with_memory_space_constraint(col_moment, pltpu.HBM),
    )
    parts = next(n for n in (9, 6, 4, 3, 2, 1) if n == 1 or rows % (n * 16) == 0)
    return pl.pallas_call(
        functools.partial(update_kernel, rows // parts),
        out_shape=(
            jax.ShapeDtypeStruct((rows, width), bf16),
            jax.ShapeDtypeStruct((rows,), f32),
            jax.ShapeDtypeStruct((width,), f32),
        ),
        in_specs=[vmem] * 5,
        out_specs=(hbm,) * 3,
        scratch_shapes=[
            pltpu.VMEM((rows, width), bf16),
            pltpu.VMEM((rows,), f32),
            pltpu.VMEM((width,), f32),
            dma((parts + 2,)),
        ],
        compiler_params=pltpu.CompilerParams(vmem_limit_bytes=24 * 1024 * 1024),
    )(grad, by_row, by_col, new_row, new_col)


def solution(mesh):
    nout, nz, ncol = mesh.shape["outer"], mesh.shape["row"], mesh.shape["col"]
    return jax.shard_map(
        functools.partial(body, nout, nz, ncol),
        mesh=mesh,
        in_specs=(
            P(("outer", "col"), "row"),
            P(("outer", "row"), "col"),
            P(("row", "outer")),
            P("col"),
        ),
        out_specs=(P(("row", "outer"), "col"), P(("row", "outer")), P("col")),
        check_vma=False,
    )
```

```python
import functools

import jax
import jax.numpy as jnp
from jax import lax
from jax.experimental import pallas as pl
from jax.experimental.pallas import tpu as pltpu
from jax.sharding import PartitionSpec as P

D = 9216
F = 8192
STEP = 2
MESH = pl.DeviceIdType.MESH


def cuts(width):
    unit = width // 128
    share, *edges = [unit * e // 32 * 128 for e in (7, 8, 16, 24, 30, 32)]
    fine = [(a, b - a) for a, b in zip([0] + edges[:-1], edges)]
    chain = [[0, 1], [2], [3, 4]]
    by_y = (0, share)
    by_z = [(share, edges[0] - share)] + fine[1:]
    return fine, chain, by_y, by_z


def each(first, last, f):
    if last - first <= 32:
        for k in range(first, last):
            f(k)
    else:
        pl.loop(first, last)(f)


def kernel(
    nout, nz, ncol, scale, decay,
    raw_ref, g_ref, rm_hbm, cm_hbm,
    acc, nr_ref, byrow_ref, nc_ref, bycol_ref,
    gs, av, raw, a_ref, rm_ref, cm_ref, rowp, early, earlyz, late, others, rowbuf,
    gz_recv, gy_recv, far_recv, mate_recv, op_recv, od_recv, a1_recv, a2_recv,
    g_send, p_send, a_send, loc_sem,
    e_sem, ez_sem, l_sem, o_sem, r_sem, ready,
):
    tg, width = g_ref.shape
    rows, ta = av.shape[1], av.shape[2]
    fine, chain, by_y, by_z = cuts(width)
    last = len(fine) - 1
    wide = early.shape[2]
    o = lax.axis_index("outer")
    z = lax.axis_index("row")
    x = lax.axis_index("col")
    y, core = o // 2, o % 2
    oy = (1 - y) * 2 + core
    op = y * 2 + (1 - core)
    od = (1 - y) * 2 + (1 - core)
    mate = z + 1 - 2 * (z % 2)
    end = jnp.where(z < nz // 2, nz - 1, 0)
    up = {"row": jnp.minimum(z + 1, nz - 1)}
    down = {"row": jnp.maximum(z - 1, 0)}

    def remote(src, dst, s, r, dev):
        return pltpu.make_async_remote_copy(
            src_ref=src, dst_ref=dst, send_sem=s, recv_sem=r, device_id=dev, device_id_type=MESH
        )

    def settle(ref, sem):
        pltpu.make_async_copy(ref, ref, sem).wait()

    load_a = pltpu.make_async_copy(raw_ref, raw, loc_sem.at[1])
    load_a.start()
    load_rm = pltpu.make_async_copy(rm_hbm, rm_ref, loc_sem.at[0])
    load_cm = pltpu.make_async_copy(cm_hbm, cm_ref, loc_sem.at[1])
    barrier = pltpu.get_barrier_semaphore()
    for who in (oy, op):
        pl.semaphore_signal(barrier, inc=1, device_id={"outer": who}, device_id_type=MESH)

    @pl.when(z > 0)
    def _():
        pl.semaphore_signal(barrier, inc=1, device_id=down, device_id_type=MESH)

    @pl.when(z < nz - 1)
    def _():
        pl.semaphore_signal(barrier, inc=1, device_id=up, device_id_type=MESH)

    for d in range(1, ncol):
        pl.semaphore_signal(barrier, inc=1, device_id={"col": (x + d) % ncol}, device_id_type=MESH)
    ends = jnp.where(z > 0, 1, 0) + jnp.where(z < nz - 1, 1, 0)
    pl.semaphore_wait(barrier, ncol + 1 + ends)

    def slots(oo, zz, count, cols):
        start = pl.multiple_of((oo * nz + zz) * tg, tg)
        return gs.at[pl.ds(start, count * tg), pl.ds(*cols)]

    def place(oo, zz, cols):
        return slots(oo, zz, 1, cols)

    def merged(c):
        first, end = fine[chain[c][0]], fine[chain[c][-1]]
        return (first[0], end[0] + end[1] - first[0])

    full = (0, width)

    def from_z(zz, c, at):
        return gz_recv.at[(zz - at - 1 + 2 * nz) % nz, c]

    def to_up(src, zz, c):
        return remote(src, place(o, zz, merged(c)), g_send, from_z(zz, c, z + 1), up)

    def to_down(src, zz, c):
        return remote(src, place(o, zz, merged(c)), g_send, from_z(zz, c, z - 1), down)

    def to_y(src, zz, cols, sem, got):
        return remote(src, place(o, zz, cols), sem, got, {"outer": oy})

    def near(src, zz, c):
        return remote(src, place(o, zz, merged(c)), p_send, op_recv.at[c], {"outer": op})

    def over(zz, cols, h):
        here = place(oy, zz, cols)
        return remote(here, here, p_send, od_recv.at[h], {"outer": op})

    for c in range(len(chain)):
        own = g_ref.at[:, pl.ds(*merged(c))]

        @pl.when(z < nz - 1)
        def _():
            to_up(own, z, c).start()

        @pl.when(z > 0)
        def _():
            to_down(own, z, c).start()

        if c == 0:
            to_y(g_ref, z, full, g_send, gy_recv.at[z]).start()
        near(own, z, c).start()

    def a_got(source, target):
        return a1_recv.at[(target - source + nout) % nout - 1]

    def a_first(target):
        return remote(a_ref.at[target], av.at[o * ncol + x], a_send, a_got(o, target), {"outer": target})

    def a_second(oo, d, own=False):
        k = oo * ncol + x
        return remote(a_ref.at[o] if own else av.at[k], av.at[k], a_send, a2_recv, {"col": (x + d) % ncol})

    local_g = pltpu.make_async_copy(g_ref, slots(o, z, 1, full), loc_sem.at[0])
    local_a = pltpu.make_async_copy(a_ref.at[o], av.at[o * ncol + x], loc_sem.at[1])
    local_g.start()
    load_a.wait()
    turned = jnp.transpose(raw[...])
    for k in range(nout):
        a_ref[k] = turned[k * rows : (k + 1) * rows]

    def pass_on(oo):
        k = oo * ncol + x
        remote(av.at[k], av.at[k], a_send, a_got(oo, o), {"outer": oy}).wait_recv()
        for d in range(1, ncol):
            a_second(oo, d).start()

    def landed(zz, cols, sem):
        here = place(oy, zz, cols)
        remote(here, here, g_send, sem, {"outer": oy}).wait_recv()

    def take_whole(zz):
        landed(zz, full, gy_recv.at[zz])
        for h in range(len(fine)):
            over(zz, fine[h], h).start()

    def take(h):
        landed(end, fine[h], far_recv.at[h])
        over(end, fine[h], h).start()
        landed(mate, fine[h], mate_recv.at[h])
        over(mate, fine[h], h).start()

    def relay(zz, c, onward):
        here = place(o, zz, merged(c))
        remote(here, here, g_send, from_z(zz, c, z), up).wait_recv()
        onward(here)

        @pl.when((zz != mate) & (zz != end))
        def _():
            to_y(here, zz, merged(c), g_send, gy_recv.at[zz]).start()

        @pl.when(zz == end)
        def _():
            for j in chain[c]:
                to_y(place(o, zz, fine[j]), zz, fine[j], g_send, far_recv.at[j]).start()

        if c == 0:
            @pl.when(zz == mate)
            def _():
                to_y(place(o, zz, by_y), zz, by_y, g_send, mate_recv.at[0]).start()

        near(here, zz, c).start()

    def extra():
        for h in range(len(fine)):
            here = place(oy, z, by_z[h])

            @pl.when(mate > z)
            def _():
                remote(here, here, g_send, mate_recv.at[h], up).start()

            @pl.when(mate < z)
            def _():
                remote(here, here, g_send, mate_recv.at[h], down).start()

    def dots(oo, cols):
        total = None
        for k in range(ncol):
            block = oo * ncol + k
            part = jnp.dot(
                av[block],
                gs[pl.ds(pl.multiple_of(block * ta, ta), ta), cols],
                preferred_element_type=jnp.float32,
            )
            total = part if total is None else total + part
        return total

    def tiles(cols, f):
        start, size = cols
        tile = 512 if size % 512 == 0 else size

        @pl.loop(0, size // tile)
        def _(j):
            f(pl.multiple_of(j * tile, 128), tile)

    def first_half(c):
        slots_here = slots(op, 0, nz, merged(c))
        remote(slots_here, slots_here, p_send, op_recv.at[c], {"outer": op}).wait_recv()
        base = merged(c)[0]

        def one(offset, tile):
            cols = pl.ds(pl.multiple_of(base + offset, 128), tile)
            acc[:, cols] = dots(o, cols) + dots(op, cols)

        tiles(merged(c), one)

    def whole_from(d):
        for zz in (z - d, z + d):
            @pl.when((zz >= 0) & (zz < nz) & (zz != mate) & (zz != end))
            def _():
                take_whole(zz)

    for s in range(1, nz):
        if s == nz - 1:
            local_g.wait()
            local_a.wait()
            load_rm.start()
            load_cm.start()
            settle(av.at[pl.ds(0, (ncol - 1) * nout)], a2_recv)
        for c in range(len(chain)):
            @pl.when(z - s >= 0)
            def _():
                def onward(here):
                    @pl.when(z < nz - 1)
                    def _():
                        to_up(here, z - s, c).start()

                relay(z - s, c, onward)

            @pl.when(z + s < nz)
            def _():
                def onward(here):
                    @pl.when(z > 0)
                    def _():
                        to_down(here, z + s, c).start()

                relay(z + s, c, onward)

            if s == 1 and c == 0:
                a_first(op).start()
                a_first(oy).start()
                for d in range(1, ncol):
                    a_second(o, d, True).start()
                local_a.start()
            if s == 1 and c == 1:
                pass_on(op)
                a_first(od).start()
            if s == nz - 1:
                first_half(c)
                if c == len(chain) - 2:
                    for d in (nz - 2, nz - 1):
                        whole_from(d)

        if s == 1:
            take_whole(z)
        if s == min(2, nz - 1):
            for c in range(2):
                pass_on((1 - y) * 2 + c)
        if s == max(nz - 2, 1):
            extra()
        if 1 < s < nz - 1:
            whole_from(s - 1)

    rowp[...] = jnp.zeros_like(rowp)
    load_rm.wait()
    load_cm.wait()
    old = rm_ref[...].reshape(1, rows)
    old_share = jnp.broadcast_to(jnp.sum(old, axis=1, keepdims=True) * (decay / ncol / 128), (1, 128))

    def finish(h, split=False):
        begin, size = fine[h]
        sums, shift = (early, 0) if begin < wide else (late, wide)

        def od_wait():
            here = slots(od, 0, nz, fine[h])
            remote(here, here, p_send, od_recv.at[h], {"outer": op}).wait_recv()

        def one(offset, tile):
            cols = pl.ds(pl.multiple_of(begin + offset, 128), tile)
            there = pl.ds(pl.multiple_of(begin - shift + offset, 128), tile)
            grad = (acc[:, cols] + dots(od, cols)) * scale if split else (acc[:, cols] + (dots(oy, cols) + dots(od, cols))) * scale
            acc[:, cols] = grad
            squares = grad * grad
            part = squares[:, :128]
            for i in range(1, tile // 128):
                part = part + squares[:, i * 128 : (i + 1) * 128]
            rowp[...] += part
            sums[0, :, there] = jnp.sum(squares, axis=0, keepdims=True)

        def ahead(offset, tile):
            cols = pl.ds(pl.multiple_of(begin + offset, 128), tile)
            acc[:, cols] = acc[:, cols] + dots(oy, cols)

        if split:
            tiles(fine[h], ahead)
        od_wait()
        tiles(fine[h], one)

    def e_first(d):
        return remote(early.at[0], early.at[nout - d], e_sem.at[0], e_sem.at[1], {"outer": (o + d) % nout})

    def e_second(d):
        return remote(earlyz.at[0], earlyz.at[nz - d], ez_sem.at[0], ez_sem.at[1], {"row": (z + d) % nz})

    @pl.when(core == 1)
    def _():
        take(0)

    for h in range(len(fine)):
        @pl.when(core == 0)
        def _():
            take(h)

        if h < last:
            @pl.when(core == 1)
            def _():
                take(h + 1)

        finish(h, h == last)
        if fine[h][0] + fine[h][1] == wide:
            for d in range(1, nout):
                e_first(d).start()
            for d in range(1, ncol):
                pl.semaphore_signal(ready, inc=1, device_id={"col": (x + d) % ncol}, device_id_type=MESH)

    group = nout * nz
    rest = width - wide

    def mirror(k):
        return ((nout - k // nz) % nout) * nz + (nz - k % nz) % nz

    def peer(k, c):
        return {"outer": (o + k // nz) % nout, "row": (z + k % nz) % nz, "col": (x + c) % ncol}

    def send_late(k):
        remote(late.at[0], late.at[mirror(k)], l_sem.at[0], l_sem.at[1], peer(k, 0)).start()

    late[0, :, pl.ds(rest, 128)] = jnp.sum(rowp[...], axis=0, keepdims=True) * ((1.0 - decay) / F) + old_share
    pl.semaphore_wait(ready, ncol - 1)
    for d in range(1, ncol):
        def send_other(k):
            slot = (ncol - d - 1) * group + mirror(k)
            remote(late.at[0, :, pl.ds(rest, 128)], others.at[slot], o_sem.at[0], o_sem.at[1], peer(k, d)).start()

        each(0, group, send_other)
    each(1, group, send_late)
    settle(early.at[pl.ds(1, nout - 1)], e_sem.at[1])
    earlyz[0] = jnp.sum(early[...], axis=0)
    for d in range(1, nz):
        e_second(d).start()
    rowbuf[0] = jnp.sum(jnp.transpose(rowp[...]), axis=0, keepdims=True)

    def r_first(d):
        return remote(rowbuf.at[0], rowbuf.at[ncol - d], r_sem.at[0], r_sem.at[1], {"col": (x + d) % ncol})

    for d in range(1, ncol):
        r_first(d).start()
    settle(rowbuf.at[pl.ds(1, ncol - 1)], r_sem.at[1])
    row_sq = jnp.sum(rowbuf[...], axis=0)
    new_row = decay * old + (1.0 - decay) * row_sq / F
    nr_ref[...] = new_row
    byrow_ref[...] = jnp.transpose(jnp.broadcast_to(lax.rsqrt(new_row), (128, rows)))
    settle(earlyz.at[pl.ds(1, nz - 1)], ez_sem.at[1])
    cm = cm_ref[...].reshape(1, width)
    new_early = decay * cm[:, :wide] + (1.0 - decay) * jnp.sum(earlyz[...], axis=0) / D
    nc_ref[:, :wide] = new_early
    settle(late.at[pl.ds(1, group - 1)], l_sem.at[1])
    arrived = jnp.sum(late[...], axis=0)
    new_late = decay * cm[:, wide:] + (1.0 - decay) * arrived[:, :rest] / D
    nc_ref[:, wide:] = new_late
    roots = [lax.rsqrt(new_early), lax.rsqrt(new_late)]
    settle(others, o_sem.at[1])
    total = jnp.sum(arrived[:, rest:] + jnp.sum(others[...], axis=0), axis=1, keepdims=True)
    root = lax.rsqrt(D / total)
    bycol_ref[:, :wide] = roots[0] * root
    bycol_ref[:, wide:] = roots[1] * root

    at_end = (z == 0) | (z == nz - 1)

    @pl.when(at_end)
    def _():
        settle(slots(0, 0, nz + 1, full), g_send)

    @pl.when(jnp.logical_not(at_end))
    def _():
        settle(slots(0, 0, 2 * nz + 1, full), g_send)

    settle(slots(0, 0, 2 * nz, full), p_send)
    settle(av.at[pl.ds(0, ncol * nout - 1)], a_send)
    settle(early.at[pl.ds(1, nout - 1)], e_sem.at[0])
    settle(earlyz.at[pl.ds(1, nz - 1)], ez_sem.at[0])
    settle(late.at[pl.ds(1, group - 1)], l_sem.at[0])
    settle(others, o_sem.at[0])
    settle(rowbuf.at[pl.ds(1, ncol - 1)], r_sem.at[0])


def update_kernel(step, grad_ref, byrow_ref, bycol_ref, nr_ref, nc_ref, out_hbm, row_hbm, col_hbm, out, row, col, sem):
    parts = out.shape[0] // step
    row[...] = nr_ref[...].reshape(row.shape)
    col[...] = nc_ref[...].reshape(col.shape)
    copies = [
        pltpu.make_async_copy(row, row_hbm, sem.at[parts]),
        pltpu.make_async_copy(col, col_hbm, sem.at[parts + 1]),
    ]
    for c in copies:
        c.start()
    for k in range(parts):
        here = pl.ds(k * step, step)
        out[here, :] = (grad_ref[here, :] * jnp.tile(byrow_ref[here, :], (1, out.shape[1] // 128)) * bycol_ref[...]).astype(out.dtype)
        copies.append(pltpu.make_async_copy(out.at[here], out_hbm.at[here], sem.at[k]))
        copies[-1].start()
    for c in copies:
        c.wait()


def body(nout, nz, ncol, activations, out_grads, row_moment, col_moment):
    rows, width = row_moment.shape[0], col_moment.shape[0]
    ta, tg = activations.shape[0], out_grads.shape[0]
    tokens = ta * ncol * nout
    decay = 1.0 - STEP ** (-0.8)
    f32, bf16 = jnp.float32, jnp.bfloat16
    vmem = pl.BlockSpec(memory_space=pltpu.VMEM)
    hbm = pl.BlockSpec(memory_space=pl.ANY)
    dma = pltpu.SemaphoreType.DMA
    fine, chain, _, _ = cuts(width)
    wide = fine[2][0] + fine[2][1]
    grad, new_row, by_row, new_col, by_col = pl.pallas_call(
        functools.partial(kernel, nout, nz, ncol, 1.0 / tokens**0.5, decay),
        out_shape=(
            pltpu.VMEM((rows, width), f32),
            pltpu.VMEM((1, rows), f32),
            pltpu.VMEM((rows, 128), f32),
            pltpu.VMEM((1, width), f32),
            pltpu.VMEM((1, width), f32),
        ),
        in_specs=[hbm] * 4,
        out_specs=(vmem,) * 5,
        scratch_shapes=[
            pltpu.VMEM((tokens, width), bf16),
            pltpu.VMEM((nout * ncol, rows, ta), bf16),
            pltpu.VMEM(activations.shape, bf16),
            pltpu.VMEM((nout, rows, ta), bf16),
            pltpu.VMEM((rows,), f32),
            pltpu.VMEM((width,), f32),
            pltpu.VMEM((rows, 128), f32),
            pltpu.VMEM((nout, 1, wide), f32),
            pltpu.VMEM((nz, 1, wide), f32),
            pltpu.VMEM((nout * nz, 1, width - wide + 128), f32),
            pltpu.VMEM(((ncol - 1) * nout * nz, 1, 128), f32),
            pltpu.VMEM((ncol, 1, rows), f32),
            dma((nz - 1, len(chain))),
            dma((nz,)),
            dma((len(fine),)),
            dma((len(fine),)),
            dma((len(chain),)),
            dma((len(fine),)),
            dma((nout - 1,)),
            dma(()),
            dma(()),
            dma(()),
            dma(()),
            dma((2,)),
            dma((2,)), dma((2,)), dma((2,)), dma((2,)), dma((2,)),
            pltpu.SemaphoreType.REGULAR,
        ],
        compiler_params=pltpu.CompilerParams(
            collective_id=0, has_side_effects=True, vmem_limit_bytes=44 * 1024 * 1024
        ),
    )(
        activations,
        out_grads,
        pltpu.with_memory_space_constraint(row_moment, pltpu.HBM),
        pltpu.with_memory_space_constraint(col_moment, pltpu.HBM),
    )
    parts = next(n for n in (9, 6, 4, 3, 2, 1) if n == 1 or rows % (n * 16) == 0)
    return pl.pallas_call(
        functools.partial(update_kernel, rows // parts),
        out_shape=(
            jax.ShapeDtypeStruct((rows, width), bf16),
            jax.ShapeDtypeStruct((rows,), f32),
            jax.ShapeDtypeStruct((width,), f32),
        ),
        in_specs=[vmem] * 5,
        out_specs=(hbm,) * 3,
        scratch_shapes=[
            pltpu.VMEM((rows, width), bf16),
            pltpu.VMEM((rows,), f32),
            pltpu.VMEM((width,), f32),
            dma((parts + 2,)),
        ],
        compiler_params=pltpu.CompilerParams(vmem_limit_bytes=24 * 1024 * 1024),
    )(grad, by_row, by_col, new_row, new_col)


def solution(mesh):
    nout, nz, ncol = mesh.shape["outer"], mesh.shape["row"], mesh.shape["col"]
    return jax.shard_map(
        functools.partial(body, nout, nz, ncol),
        mesh=mesh,
        in_specs=(
            P(("outer", "col"), "row"),
            P(("outer", "row"), "col"),
            P(("row", "outer")),
            P("col"),
        ),
        out_specs=(P(("row", "outer"), "col"), P(("row", "outer")), P("col")),
        check_vma=False,
    )
```

```python
import functools

import jax
import jax.numpy as jnp
from jax import lax
from jax.experimental import pallas as pl
from jax.experimental.pallas import tpu as pltpu
from jax.sharding import PartitionSpec as P

D = 9216
F = 8192
STEP = 2
MESH = pl.DeviceIdType.MESH


def cuts(width):
    unit = width // 128
    share, *edges = [unit * e // 32 * 128 for e in (7, 8, 16, 24, 28, 32)]
    fine = [(a, b - a) for a, b in zip([0] + edges[:-1], edges)]
    chain = [[0, 1], [2], [3, 4]]
    by_y = (0, share)
    by_z = [(share, edges[0] - share)] + fine[1:]
    return fine, chain, by_y, by_z


def each(first, last, f):
    if last - first <= 32:
        for k in range(first, last):
            f(k)
    else:
        pl.loop(first, last)(f)


def kernel(
    nout, nz, ncol, scale, decay,
    raw_ref, g_ref, rm_hbm, cm_hbm,
    acc, nr_ref, byrow_ref, nc_ref, bycol_ref,
    gs, av, raw, a_ref, rm_ref, cm_ref, rowp, early, earlyz, late, others, rowbuf,
    gz_recv, gy_recv, far_recv, mate_recv, op_recv, od_recv, a1_recv, a2_recv,
    g_send, p_send, a_send, loc_sem,
    e_sem, ez_sem, l_sem, o_sem, r_sem, ready,
):
    tg, width = g_ref.shape
    rows, ta = av.shape[1], av.shape[2]
    fine, chain, by_y, by_z = cuts(width)
    last = len(fine) - 1
    wide = early.shape[2]
    o = lax.axis_index("outer")
    z = lax.axis_index("row")
    x = lax.axis_index("col")
    y, core = o // 2, o % 2
    oy = (1 - y) * 2 + core
    op = y * 2 + (1 - core)
    od = (1 - y) * 2 + (1 - core)
    mate = z + 1 - 2 * (z % 2)
    end = jnp.where(z < nz // 2, nz - 1, 0)
    up = {"row": jnp.minimum(z + 1, nz - 1)}
    down = {"row": jnp.maximum(z - 1, 0)}

    def remote(src, dst, s, r, dev):
        return pltpu.make_async_remote_copy(
            src_ref=src, dst_ref=dst, send_sem=s, recv_sem=r, device_id=dev, device_id_type=MESH
        )

    def settle(ref, sem):
        pltpu.make_async_copy(ref, ref, sem).wait()

    def slots(oo, zz, count, cols):
        start = pl.multiple_of((oo * nz + zz) * tg, tg)
        return gs.at[pl.ds(start, count * tg), pl.ds(*cols)]

    def place(oo, zz, cols):
        return slots(oo, zz, 1, cols)

    full = (0, width)
    local_g = pltpu.make_async_copy(g_ref, slots(o, z, 1, full), loc_sem.at[0])
    load_a = pltpu.make_async_copy(raw_ref, raw, loc_sem.at[1])
    local_g.start()
    load_a.start()
    load_rm = pltpu.make_async_copy(rm_hbm, rm_ref, loc_sem.at[0])
    load_cm = pltpu.make_async_copy(cm_hbm, cm_ref, loc_sem.at[1])
    barrier = pltpu.get_barrier_semaphore()
    for who in (oy, op):
        pl.semaphore_signal(barrier, inc=1, device_id={"outer": who}, device_id_type=MESH)

    @pl.when(z > 0)
    def _():
        pl.semaphore_signal(barrier, inc=1, device_id=down, device_id_type=MESH)

    @pl.when(z < nz - 1)
    def _():
        pl.semaphore_signal(barrier, inc=1, device_id=up, device_id_type=MESH)

    for d in range(1, ncol):
        pl.semaphore_signal(barrier, inc=1, device_id={"col": (x + d) % ncol}, device_id_type=MESH)
    ends = jnp.where(z > 0, 1, 0) + jnp.where(z < nz - 1, 1, 0)
    pl.semaphore_wait(barrier, ncol + 1 + ends)

    def merged(c):
        first, end = fine[chain[c][0]], fine[chain[c][-1]]
        return (first[0], end[0] + end[1] - first[0])

    def from_z(zz, c, at):
        return gz_recv.at[(zz - at - 1 + 2 * nz) % nz, c]

    def to_up(src, zz, c):
        return remote(src, place(o, zz, merged(c)), g_send, from_z(zz, c, z + 1), up)

    def to_down(src, zz, c):
        return remote(src, place(o, zz, merged(c)), g_send, from_z(zz, c, z - 1), down)

    def to_y(src, zz, cols, sem, got):
        return remote(src, place(o, zz, cols), sem, got, {"outer": oy})

    def near(src, zz, c):
        return remote(src, place(o, zz, merged(c)), p_send, op_recv.at[c], {"outer": op})

    def over(zz, cols, h):
        here = place(oy, zz, cols)
        return remote(here, here, p_send, od_recv.at[h], {"outer": op})

    local_g.wait()
    for c in range(len(chain)):
        own = place(o, z, merged(c))

        @pl.when(z < nz - 1)
        def _():
            to_up(own, z, c).start()

        @pl.when(z > 0)
        def _():
            to_down(own, z, c).start()

        if c == 0:
            to_y(place(o, z, full), z, full, g_send, gy_recv.at[z]).start()
        near(own, z, c).start()

    def a_got(source, target):
        return a1_recv.at[(target - source + nout) % nout - 1]

    def a_first(target):
        return remote(a_ref.at[target], av.at[o * ncol + x], a_send, a_got(o, target), {"outer": target})

    def a_second(oo, d, own=False):
        k = oo * ncol + x
        return remote(a_ref.at[o] if own else av.at[k], av.at[k], a_send, a2_recv, {"col": (x + d) % ncol})

    local_a = pltpu.make_async_copy(a_ref.at[o], av.at[o * ncol + x], loc_sem.at[1])
    load_a.wait()
    turned = jnp.transpose(raw[...])
    for k in range(nout):
        a_ref[k] = turned[k * rows : (k + 1) * rows]

    def pass_on(oo):
        k = oo * ncol + x
        remote(av.at[k], av.at[k], a_send, a_got(oo, o), {"outer": oy}).wait_recv()
        for d in range(1, ncol):
            a_second(oo, d).start()

    def landed(zz, cols, sem):
        here = place(oy, zz, cols)
        remote(here, here, g_send, sem, {"outer": oy}).wait_recv()

    def take_whole(zz):
        landed(zz, full, gy_recv.at[zz])
        for h in range(len(fine)):
            over(zz, fine[h], h).start()

    def take(h):
        landed(end, fine[h], far_recv.at[h])
        over(end, fine[h], h).start()
        landed(mate, fine[h], mate_recv.at[h])
        over(mate, fine[h], h).start()

    def relay(zz, c, onward):
        here = place(o, zz, merged(c))
        remote(here, here, g_send, from_z(zz, c, z), up).wait_recv()
        onward(here)

        @pl.when((zz != mate) & (zz != end))
        def _():
            to_y(here, zz, merged(c), g_send, gy_recv.at[zz]).start()

        @pl.when(zz == end)
        def _():
            for j in chain[c]:
                to_y(place(o, zz, fine[j]), zz, fine[j], g_send, far_recv.at[j]).start()

        if c == 0:
            @pl.when(zz == mate)
            def _():
                to_y(place(o, zz, by_y), zz, by_y, g_send, mate_recv.at[0]).start()

        near(here, zz, c).start()

    def extra():
        for h in range(len(fine)):
            here = place(oy, z, by_z[h])

            @pl.when(mate > z)
            def _():
                remote(here, here, g_send, mate_recv.at[h], up).start()

            @pl.when(mate < z)
            def _():
                remote(here, here, g_send, mate_recv.at[h], down).start()

    def dots(oo, cols):
        total = None
        for k in range(ncol):
            block = oo * ncol + k
            part = jnp.dot(
                av[block],
                gs[pl.ds(pl.multiple_of(block * ta, ta), ta), cols],
                preferred_element_type=jnp.float32,
            )
            total = part if total is None else total + part
        return total

    def tiles(cols, f):
        start, size = cols
        tile = 512 if size % 512 == 0 else size

        @pl.loop(0, size // tile)
        def _(j):
            f(pl.multiple_of(j * tile, 128), tile)

    def first_half(c):
        slots_here = slots(op, 0, nz, merged(c))
        remote(slots_here, slots_here, p_send, op_recv.at[c], {"outer": op}).wait_recv()
        base = merged(c)[0]

        def one(offset, tile):
            cols = pl.ds(pl.multiple_of(base + offset, 128), tile)
            acc[:, cols] = dots(o, cols) + dots(op, cols)

        tiles(merged(c), one)

    def whole_from(d):
        for zz in (z - d, z + d):
            @pl.when((zz >= 0) & (zz < nz) & (zz != mate) & (zz != end))
            def _():
                take_whole(zz)

    for s in range(1, nz):
        if s == nz - 1:
            local_a.wait()
            load_rm.start()
            load_cm.start()
            settle(av.at[pl.ds(0, (ncol - 1) * nout)], a2_recv)
        for c in range(len(chain)):
            @pl.when(z - s >= 0)
            def _():
                def onward(here):
                    @pl.when(z < nz - 1)
                    def _():
                        to_up(here, z - s, c).start()

                relay(z - s, c, onward)

            @pl.when(z + s < nz)
            def _():
                def onward(here):
                    @pl.when(z > 0)
                    def _():
                        to_down(here, z + s, c).start()

                relay(z + s, c, onward)

            if s == 1 and c == 0:
                a_first(op).start()
                a_first(oy).start()
                for d in range(1, ncol):
                    a_second(o, d, True).start()
                local_a.start()
            if s == 1 and c == 1:
                pass_on(op)
                a_first(od).start()
            if s == nz - 1:
                first_half(c)
                if c == len(chain) - 2:
                    for d in (nz - 2, nz - 1):
                        whole_from(d)

        if s == 1:
            take_whole(z)
        if s == min(2, nz - 1):
            for c in range(2):
                pass_on((1 - y) * 2 + c)
        if s == max(nz - 2, 1):
            extra()
        if 1 < s < nz - 1:
            whole_from(s - 1)

    rowp[...] = jnp.zeros_like(rowp)
    load_rm.wait()
    load_cm.wait()
    old = rm_ref[...].reshape(1, rows)
    old_share = jnp.broadcast_to(jnp.sum(old, axis=1, keepdims=True) * (decay / ncol / 128), (1, 128))

    def finish(h, split=False):
        begin, size = fine[h]
        sums, shift = (early, 0) if begin < wide else (late, wide)

        def od_wait():
            here = slots(od, 0, nz, fine[h])
            remote(here, here, p_send, od_recv.at[h], {"outer": op}).wait_recv()

        def one(offset, tile):
            cols = pl.ds(pl.multiple_of(begin + offset, 128), tile)
            there = pl.ds(pl.multiple_of(begin - shift + offset, 128), tile)
            grad = (acc[:, cols] + dots(od, cols)) * scale if split else (acc[:, cols] + (dots(oy, cols) + dots(od, cols))) * scale
            acc[:, cols] = grad
            squares = grad * grad
            part = squares[:, :128]
            for i in range(1, tile // 128):
                part = part + squares[:, i * 128 : (i + 1) * 128]
            rowp[...] += part
            sums[0, :, there] = jnp.sum(squares, axis=0, keepdims=True)

        def ahead(offset, tile):
            cols = pl.ds(pl.multiple_of(begin + offset, 128), tile)
            acc[:, cols] = acc[:, cols] + dots(oy, cols)

        if split:
            tiles(fine[h], ahead)
        od_wait()
        tiles(fine[h], one)

    def e_first(d):
        return remote(early.at[0], early.at[nout - d], e_sem.at[0], e_sem.at[1], {"outer": (o + d) % nout})

    def e_second(d):
        return remote(earlyz.at[0], earlyz.at[nz - d], ez_sem.at[0], ez_sem.at[1], {"row": (z + d) % nz})

    @pl.when(core == 1)
    def _():
        take(0)

    for h in range(len(fine)):
        @pl.when(core == 0)
        def _():
            take(h)

        if h < last:
            @pl.when(core == 1)
            def _():
                take(h + 1)

        finish(h, h == last)
        if fine[h][0] + fine[h][1] == wide:
            for d in range(1, nout):
                e_first(d).start()
            for d in range(1, ncol):
                pl.semaphore_signal(ready, inc=1, device_id={"col": (x + d) % ncol}, device_id_type=MESH)

    group = nout * nz
    rest = width - wide

    def mirror(k):
        return ((nout - k // nz) % nout) * nz + (nz - k % nz) % nz

    def peer(k, c):
        return {"outer": (o + k // nz) % nout, "row": (z + k % nz) % nz, "col": (x + c) % ncol}

    def send_late(k):
        remote(late.at[0], late.at[mirror(k)], l_sem.at[0], l_sem.at[1], peer(k, 0)).start()

    late[0, :, pl.ds(rest, 128)] = jnp.sum(rowp[...], axis=0, keepdims=True) * ((1.0 - decay) / F) + old_share
    pl.semaphore_wait(ready, ncol - 1)
    for d in range(1, ncol):
        def send_other(k):
            slot = (ncol - d - 1) * group + mirror(k)
            remote(late.at[0, :, pl.ds(rest, 128)], others.at[slot], o_sem.at[0], o_sem.at[1], peer(k, d)).start()

        each(0, group, send_other)
    each(1, group, send_late)
    settle(early.at[pl.ds(1, nout - 1)], e_sem.at[1])
    earlyz[0] = jnp.sum(early[...], axis=0)
    for d in range(1, nz):
        e_second(d).start()
    rowbuf[0] = jnp.sum(jnp.transpose(rowp[...]), axis=0, keepdims=True)

    def r_first(d):
        return remote(rowbuf.at[0], rowbuf.at[ncol - d], r_sem.at[0], r_sem.at[1], {"col": (x + d) % ncol})

    for d in range(1, ncol):
        r_first(d).start()
    settle(rowbuf.at[pl.ds(1, ncol - 1)], r_sem.at[1])
    row_sq = jnp.sum(rowbuf[...], axis=0)
    new_row = decay * old + (1.0 - decay) * row_sq / F
    nr_ref[...] = new_row
    byrow_ref[...] = jnp.transpose(jnp.broadcast_to(lax.rsqrt(new_row), (128, rows)))
    settle(earlyz.at[pl.ds(1, nz - 1)], ez_sem.at[1])
    cm = cm_ref[...].reshape(1, width)
    new_early = decay * cm[:, :wide] + (1.0 - decay) * jnp.sum(earlyz[...], axis=0) / D
    nc_ref[:, :wide] = new_early
    settle(late.at[pl.ds(1, group - 1)], l_sem.at[1])
    arrived = jnp.sum(late[...], axis=0)
    new_late = decay * cm[:, wide:] + (1.0 - decay) * arrived[:, :rest] / D
    nc_ref[:, wide:] = new_late
    roots = [lax.rsqrt(new_early), lax.rsqrt(new_late)]
    settle(others, o_sem.at[1])
    total = jnp.sum(arrived[:, rest:] + jnp.sum(others[...], axis=0), axis=1, keepdims=True)
    root = lax.rsqrt(D / total)
    bycol_ref[:, :wide] = roots[0] * root
    bycol_ref[:, wide:] = roots[1] * root

    at_end = (z == 0) | (z == nz - 1)

    @pl.when(at_end)
    def _():
        settle(slots(0, 0, nz + 1, full), g_send)

    @pl.when(jnp.logical_not(at_end))
    def _():
        settle(slots(0, 0, 2 * nz + 1, full), g_send)

    settle(slots(0, 0, 2 * nz, full), p_send)
    settle(av.at[pl.ds(0, ncol * nout - 1)], a_send)
    settle(early.at[pl.ds(1, nout - 1)], e_sem.at[0])
    settle(earlyz.at[pl.ds(1, nz - 1)], ez_sem.at[0])
    settle(late.at[pl.ds(1, group - 1)], l_sem.at[0])
    settle(others, o_sem.at[0])
    settle(rowbuf.at[pl.ds(1, ncol - 1)], r_sem.at[0])


def update_kernel(step, grad_ref, byrow_ref, bycol_ref, nr_ref, nc_ref, out_hbm, row_hbm, col_hbm, out, row, col, sem):
    parts = out.shape[0] // step
    row[...] = nr_ref[...].reshape(row.shape)
    col[...] = nc_ref[...].reshape(col.shape)
    copies = [
        pltpu.make_async_copy(row, row_hbm, sem.at[parts]),
        pltpu.make_async_copy(col, col_hbm, sem.at[parts + 1]),
    ]
    for c in copies:
        c.start()
    for k in range(parts):
        here = pl.ds(k * step, step)
        out[here, :] = (grad_ref[here, :] * jnp.tile(byrow_ref[here, :], (1, out.shape[1] // 128)) * bycol_ref[...]).astype(out.dtype)
        copies.append(pltpu.make_async_copy(out.at[here], out_hbm.at[here], sem.at[k]))
        copies[-1].start()
    for c in copies:
        c.wait()


def body(nout, nz, ncol, activations, out_grads, row_moment, col_moment):
    rows, width = row_moment.shape[0], col_moment.shape[0]
    ta, tg = activations.shape[0], out_grads.shape[0]
    tokens = ta * ncol * nout
    decay = 1.0 - STEP ** (-0.8)
    f32, bf16 = jnp.float32, jnp.bfloat16
    vmem = pl.BlockSpec(memory_space=pltpu.VMEM)
    hbm = pl.BlockSpec(memory_space=pl.ANY)
    dma = pltpu.SemaphoreType.DMA
    fine, chain, _, _ = cuts(width)
    wide = fine[2][0] + fine[2][1]
    grad, new_row, by_row, new_col, by_col = pl.pallas_call(
        functools.partial(kernel, nout, nz, ncol, 1.0 / tokens**0.5, decay),
        out_shape=(
            pltpu.VMEM((rows, width), f32),
            pltpu.VMEM((1, rows), f32),
            pltpu.VMEM((rows, 128), f32),
            pltpu.VMEM((1, width), f32),
            pltpu.VMEM((1, width), f32),
        ),
        in_specs=[hbm] * 4,
        out_specs=(vmem,) * 5,
        scratch_shapes=[
            pltpu.VMEM((tokens, width), bf16),
            pltpu.VMEM((nout * ncol, rows, ta), bf16),
            pltpu.VMEM(activations.shape, bf16),
            pltpu.VMEM((nout, rows, ta), bf16),
            pltpu.VMEM((rows,), f32),
            pltpu.VMEM((width,), f32),
            pltpu.VMEM((rows, 128), f32),
            pltpu.VMEM((nout, 1, wide), f32),
            pltpu.VMEM((nz, 1, wide), f32),
            pltpu.VMEM((nout * nz, 1, width - wide + 128), f32),
            pltpu.VMEM(((ncol - 1) * nout * nz, 1, 128), f32),
            pltpu.VMEM((ncol, 1, rows), f32),
            dma((nz - 1, len(chain))),
            dma((nz,)),
            dma((len(fine),)),
            dma((len(fine),)),
            dma((len(chain),)),
            dma((len(fine),)),
            dma((nout - 1,)),
            dma(()),
            dma(()),
            dma(()),
            dma(()),
            dma((2,)),
            dma((2,)), dma((2,)), dma((2,)), dma((2,)), dma((2,)),
            pltpu.SemaphoreType.REGULAR,
        ],
        compiler_params=pltpu.CompilerParams(
            collective_id=0, has_side_effects=True, vmem_limit_bytes=44 * 1024 * 1024
        ),
    )(
        activations,
        out_grads,
        pltpu.with_memory_space_constraint(row_moment, pltpu.HBM),
        pltpu.with_memory_space_constraint(col_moment, pltpu.HBM),
    )
    parts = next(n for n in (9, 6, 4, 3, 2, 1) if n == 1 or rows % (n * 16) == 0)
    return pl.pallas_call(
        functools.partial(update_kernel, rows // parts),
        out_shape=(
            jax.ShapeDtypeStruct((rows, width), bf16),
            jax.ShapeDtypeStruct((rows,), f32),
            jax.ShapeDtypeStruct((width,), f32),
        ),
        in_specs=[vmem] * 5,
        out_specs=(hbm,) * 3,
        scratch_shapes=[
            pltpu.VMEM((rows, width), bf16),
            pltpu.VMEM((rows,), f32),
            pltpu.VMEM((width,), f32),
            dma((parts + 2,)),
        ],
        compiler_params=pltpu.CompilerParams(vmem_limit_bytes=24 * 1024 * 1024),
    )(grad, by_row, by_col, new_row, new_col)


def solution(mesh):
    nout, nz, ncol = mesh.shape["outer"], mesh.shape["row"], mesh.shape["col"]
    return jax.shard_map(
        functools.partial(body, nout, nz, ncol),
        mesh=mesh,
        in_specs=(
            P(("outer", "col"), "row"),
            P(("outer", "row"), "col"),
            P(("row", "outer")),
            P("col"),
        ),
        out_specs=(P(("row", "outer"), "col"), P(("row", "outer")), P("col")),
        check_vma=False,
    )
```

```python
import functools

import jax
import jax.numpy as jnp
from jax import lax
from jax.experimental import pallas as pl
from jax.experimental.pallas import tpu as pltpu
from jax.sharding import PartitionSpec as P

D = 9216
F = 8192
STEP = 2
MESH = pl.DeviceIdType.MESH


def cuts(width):
    unit = width // 128
    share, *edges = [unit * e // 32 * 128 for e in (7, 8, 16, 24, 28, 32)]
    fine = [(a, b - a) for a, b in zip([0] + edges[:-1], edges)]
    chain = [[0, 1], [2, 3, 4]]
    by_y = (0, share)
    start, size = fine[-1]
    head = max(size // 256, 1) * 128
    lasts = [(start, head), (start + head, size - head)] if size > head else [(start, size)]
    subs = [[cols] for cols in fine[:-1]] + [lasts]
    by_z = [[(share, edges[0] - share)]] + subs[1:]
    return fine, chain, by_y, by_z, subs


def each(first, last, f):
    if last - first <= 32:
        for k in range(first, last):
            f(k)
    else:
        pl.loop(first, last)(f)


def kernel(
    nout, nz, ncol, scale, decay,
    raw_ref, g_ref, rm_hbm, cm_hbm,
    acc, nr_ref, byrow_ref, nc_ref, bycol_ref,
    gs, av, raw, a_ref, rm_ref, cm_ref, rowp, early, earlyz, late, others, rowbuf,
    gz_recv, gy_recv, last_recv, op_recv, od_recv, a1_recv, a2_recv,
    g_send, p_send, a_send, loc_sem,
    e_sem, ez_sem, l_sem, o_sem, r_sem, ready,
):
    tg, width = g_ref.shape
    rows, ta = av.shape[1], av.shape[2]
    fine, chain, by_y, by_z, subs = cuts(width)
    last = len(fine) - 1
    wide = early.shape[2]
    o = lax.axis_index("outer")
    z = lax.axis_index("row")
    x = lax.axis_index("col")
    y, core = o // 2, o % 2
    oy = (1 - y) * 2 + core
    op = y * 2 + (1 - core)
    od = (1 - y) * 2 + (1 - core)
    mate = z + 1 - 2 * (z % 2)
    end = jnp.where(z < nz // 2, nz - 1, 0)
    up = {"row": jnp.minimum(z + 1, nz - 1)}
    down = {"row": jnp.maximum(z - 1, 0)}

    def remote(src, dst, s, r, dev):
        return pltpu.make_async_remote_copy(
            src_ref=src, dst_ref=dst, send_sem=s, recv_sem=r, device_id=dev, device_id_type=MESH
        )

    def settle(ref, sem):
        pltpu.make_async_copy(ref, ref, sem).wait()

    def slots(oo, zz, count, cols):
        start = pl.multiple_of((oo * nz + zz) * tg, tg)
        return gs.at[pl.ds(start, count * tg), pl.ds(*cols)]

    def place(oo, zz, cols):
        return slots(oo, zz, 1, cols)

    full = (0, width)
    local_g = pltpu.make_async_copy(g_ref, slots(o, z, 1, full), loc_sem.at[0])
    load_a = pltpu.make_async_copy(raw_ref, raw, loc_sem.at[1])
    local_g.start()
    load_a.start()
    load_rm = pltpu.make_async_copy(rm_hbm, rm_ref, loc_sem.at[0])
    load_cm = pltpu.make_async_copy(cm_hbm, cm_ref, loc_sem.at[1])
    barrier = pltpu.get_barrier_semaphore()
    for who in (oy, op):
        pl.semaphore_signal(barrier, inc=1, device_id={"outer": who}, device_id_type=MESH)

    @pl.when(z > 0)
    def _():
        pl.semaphore_signal(barrier, inc=1, device_id=down, device_id_type=MESH)

    @pl.when(z < nz - 1)
    def _():
        pl.semaphore_signal(barrier, inc=1, device_id=up, device_id_type=MESH)

    for d in range(1, ncol):
        pl.semaphore_signal(barrier, inc=1, device_id={"col": (x + d) % ncol}, device_id_type=MESH)
    ends = jnp.where(z > 0, 1, 0) + jnp.where(z < nz - 1, 1, 0)
    pl.semaphore_wait(barrier, ncol + 1 + ends)

    def merged(c):
        first, end = fine[chain[c][0]], fine[chain[c][-1]]
        return (first[0], end[0] + end[1] - first[0])

    def from_z(zz, c, at):
        return gz_recv.at[(zz - at - 1 + 2 * nz) % nz, c]

    def to_up(src, zz, c):
        return remote(src, place(o, zz, merged(c)), g_send, from_z(zz, c, z + 1), up)

    def to_down(src, zz, c):
        return remote(src, place(o, zz, merged(c)), g_send, from_z(zz, c, z - 1), down)

    def to_y(src, zz, cols, sem, got):
        return remote(src, place(o, zz, cols), sem, got, {"outer": oy})

    def near(src, zz, c):
        return remote(src, place(o, zz, merged(c)), p_send, op_recv.at[c], {"outer": op})

    def over(zz, cols, h):
        here = place(oy, zz, cols)
        return remote(here, here, p_send, od_recv.at[h], {"outer": op})

    local_g.wait()
    for c in range(len(chain)):
        own = place(o, z, merged(c))

        @pl.when(z < nz - 1)
        def _():
            to_up(own, z, c).start()

        @pl.when(z > 0)
        def _():
            to_down(own, z, c).start()

        if c == 0:
            to_y(place(o, z, full), z, full, g_send, gy_recv.at[z]).start()
        near(own, z, c).start()

    def a_got(source, target):
        return a1_recv.at[(target - source + nout) % nout - 1]

    def a_first(target):
        return remote(a_ref.at[target], av.at[o * ncol + x], a_send, a_got(o, target), {"outer": target})

    def a_second(oo, d, own=False):
        k = oo * ncol + x
        return remote(a_ref.at[o] if own else av.at[k], av.at[k], a_send, a2_recv, {"col": (x + d) % ncol})

    local_a = pltpu.make_async_copy(a_ref.at[o], av.at[o * ncol + x], loc_sem.at[1])
    load_a.wait()
    turned = jnp.transpose(raw[...])
    for k in range(nout):
        a_ref[k] = turned[k * rows : (k + 1) * rows]

    def pass_on(oo):
        k = oo * ncol + x
        remote(av.at[k], av.at[k], a_send, a_got(oo, o), {"outer": oy}).wait_recv()
        for d in range(1, ncol):
            a_second(oo, d).start()

    def landed(zz, cols, sem):
        here = place(oy, zz, cols)
        remote(here, here, g_send, sem, {"outer": oy}).wait_recv()

    def take_whole(zz):
        landed(zz, full, gy_recv.at[zz])
        for h in range(len(fine)):
            over(zz, fine[h], h).start()

    def take(h):
        for i, cols in enumerate(subs[h]):
            both = slots(oy, 0, 2, cols)
            remote(both, both, g_send, last_recv.at[h + i], {"outer": oy}).wait_recv()
            over(end, cols, h).start()
            over(mate, cols, h).start()

    def relay(zz, c, onward):
        here = place(o, zz, merged(c))
        remote(here, here, g_send, from_z(zz, c, z), up).wait_recv()
        onward(here)

        @pl.when((zz != mate) & (zz != end))
        def _():
            to_y(here, zz, merged(c), g_send, gy_recv.at[zz]).start()

        @pl.when(zz == end)
        def _():
            for j in chain[c]:
                for i, cols in enumerate(subs[j]):
                    to_y(place(o, zz, cols), zz, cols, g_send, last_recv.at[j + i]).start()

        if c == 0:
            @pl.when(zz == mate)
            def _():
                to_y(place(o, zz, by_y), zz, by_y, g_send, last_recv.at[0]).start()

        near(here, zz, c).start()

    def extra():
        for h in range(len(fine)):
            for i, cols in enumerate(by_z[h]):
                here = place(oy, z, cols)

                @pl.when(mate > z)
                def _():
                    remote(here, here, g_send, last_recv.at[h + i], up).start()

                @pl.when(mate < z)
                def _():
                    remote(here, here, g_send, last_recv.at[h + i], down).start()

    def dots(oo, cols):
        total = None
        for k in range(ncol):
            block = oo * ncol + k
            part = jnp.dot(
                av[block],
                gs[pl.ds(pl.multiple_of(block * ta, ta), ta), cols],
                preferred_element_type=jnp.float32,
            )
            total = part if total is None else total + part
        return total

    def tiles(cols, f):
        start, size = cols
        tile = 512 if size % 512 == 0 else size

        @pl.loop(0, size // tile)
        def _(j):
            f(pl.multiple_of(j * tile, 128), tile)

    def first_half(c):
        slots_here = slots(op, 0, nz, merged(c))
        remote(slots_here, slots_here, p_send, op_recv.at[c], {"outer": op}).wait_recv()
        base = merged(c)[0]

        def one(offset, tile):
            cols = pl.ds(pl.multiple_of(base + offset, 128), tile)
            acc[:, cols] = dots(o, cols) + dots(op, cols)

        tiles(merged(c), one)

    def whole_from(d):
        for zz in (z - d, z + d):
            @pl.when((zz >= 0) & (zz < nz) & (zz != mate) & (zz != end))
            def _():
                take_whole(zz)

    for s in range(1, nz):
        if s == nz - 1:
            local_a.wait()
            load_rm.start()
            load_cm.start()
            settle(av.at[pl.ds(0, (ncol - 1) * nout)], a2_recv)
        for c in range(len(chain)):
            @pl.when(z - s >= 0)
            def _():
                def onward(here):
                    @pl.when(z < nz - 1)
                    def _():
                        to_up(here, z - s, c).start()

                relay(z - s, c, onward)

            @pl.when(z + s < nz)
            def _():
                def onward(here):
                    @pl.when(z > 0)
                    def _():
                        to_down(here, z + s, c).start()

                relay(z + s, c, onward)

            if s == 1 and c == 0:
                a_first(op).start()
                a_first(oy).start()
                for d in range(1, ncol):
                    a_second(o, d, True).start()
                local_a.start()
                pass_on(op)
                a_first(od).start()
            if s == nz - 1:
                first_half(c)
                if c == len(chain) - 2:
                    for d in (nz - 2, nz - 1):
                        whole_from(d)

        if s == 1:
            take_whole(z)
        if s == min(2, nz - 1):
            for c in range(2):
                pass_on((1 - y) * 2 + c)
        if s == max(nz - 2, 1):
            extra()
        if 1 < s < nz - 1:
            whole_from(s - 1)

    rowp[...] = jnp.zeros_like(rowp)
    load_rm.wait()
    load_cm.wait()
    old = rm_ref[...].reshape(1, rows)
    old_share = jnp.broadcast_to(jnp.sum(old, axis=1, keepdims=True) * (decay / ncol / 128), (1, 128))

    def finish(h, split=False):
        begin, size = fine[h]
        sums, shift = (early, 0) if begin < wide else (late, wide)

        def od_wait():
            here = slots(od, 0, nz, fine[h])
            remote(here, here, p_send, od_recv.at[h], {"outer": op}).wait_recv()

        def one(offset, tile):
            cols = pl.ds(pl.multiple_of(begin + offset, 128), tile)
            there = pl.ds(pl.multiple_of(begin - shift + offset, 128), tile)
            grad = (acc[:, cols] + dots(od, cols)) * scale if split else (acc[:, cols] + (dots(oy, cols) + dots(od, cols))) * scale
            acc[:, cols] = grad
            squares = grad * grad
            part = squares[:, :128]
            for i in range(1, tile // 128):
                part = part + squares[:, i * 128 : (i + 1) * 128]
            rowp[...] += part
            sums[0, :, there] = jnp.sum(squares, axis=0, keepdims=True)

        def ahead(offset, tile):
            cols = pl.ds(pl.multiple_of(begin + offset, 128), tile)
            acc[:, cols] = acc[:, cols] + dots(oy, cols)

        if split:
            tiles(fine[h], ahead)
        od_wait()
        tiles(fine[h], one)

    def e_first(d):
        return remote(early.at[0], early.at[nout - d], e_sem.at[0], e_sem.at[1], {"outer": (o + d) % nout})

    def e_second(d):
        return remote(earlyz.at[0], earlyz.at[nz - d], ez_sem.at[0], ez_sem.at[1], {"row": (z + d) % nz})

    @pl.when(core == 1)
    def _():
        take(0)

    for h in range(len(fine)):
        @pl.when(core == 0)
        def _():
            take(h)

        if h < last:
            @pl.when(core == 1)
            def _():
                take(h + 1)

        finish(h, h == last)
        if fine[h][0] + fine[h][1] == wide:
            for d in range(1, nout):
                e_first(d).start()
            for d in range(1, ncol):
                pl.semaphore_signal(ready, inc=1, device_id={"col": (x + d) % ncol}, device_id_type=MESH)

    group = nout * nz
    rest = width - wide

    def mirror(k):
        return ((nout - k // nz) % nout) * nz + (nz - k % nz) % nz

    def peer(k, c):
        return {"outer": (o + k // nz) % nout, "row": (z + k % nz) % nz, "col": (x + c) % ncol}

    def send_late(k):
        remote(late.at[0], late.at[mirror(k)], l_sem.at[0], l_sem.at[1], peer(k, 0)).start()

    late[0, :, pl.ds(rest, 128)] = jnp.sum(rowp[...], axis=0, keepdims=True) * ((1.0 - decay) / F) + old_share
    pl.semaphore_wait(ready, ncol - 1)
    for d in range(1, ncol):
        def send_other(k):
            slot = (ncol - d - 1) * group + mirror(k)
            remote(late.at[0, :, pl.ds(rest, 128)], others.at[slot], o_sem.at[0], o_sem.at[1], peer(k, d)).start()

        each(0, group, send_other)
    each(1, group, send_late)
    settle(early.at[pl.ds(1, nout - 1)], e_sem.at[1])
    earlyz[0] = jnp.sum(early[...], axis=0)
    for d in range(1, nz):
        e_second(d).start()
    rowbuf[0] = jnp.sum(jnp.transpose(rowp[...]), axis=0, keepdims=True)

    def r_first(d):
        return remote(rowbuf.at[0], rowbuf.at[ncol - d], r_sem.at[0], r_sem.at[1], {"col": (x + d) % ncol})

    for d in range(1, ncol):
        r_first(d).start()
    settle(rowbuf.at[pl.ds(1, ncol - 1)], r_sem.at[1])
    row_sq = jnp.sum(rowbuf[...], axis=0)
    new_row = decay * old + (1.0 - decay) * row_sq / F
    nr_ref[...] = new_row
    byrow_ref[...] = jnp.transpose(jnp.broadcast_to(lax.rsqrt(new_row), (128, rows)))
    settle(earlyz.at[pl.ds(1, nz - 1)], ez_sem.at[1])
    cm = cm_ref[...].reshape(1, width)
    new_early = decay * cm[:, :wide] + (1.0 - decay) * jnp.sum(earlyz[...], axis=0) / D
    nc_ref[:, :wide] = new_early
    settle(late.at[pl.ds(1, group - 1)], l_sem.at[1])
    arrived = jnp.sum(late[...], axis=0)
    new_late = decay * cm[:, wide:] + (1.0 - decay) * arrived[:, :rest] / D
    nc_ref[:, wide:] = new_late
    roots = [lax.rsqrt(new_early), lax.rsqrt(new_late)]
    settle(others, o_sem.at[1])
    total = jnp.sum(arrived[:, rest:] + jnp.sum(others[...], axis=0), axis=1, keepdims=True)
    root = lax.rsqrt(D / total)
    bycol_ref[:, :wide] = roots[0] * root
    bycol_ref[:, wide:] = roots[1] * root

    at_end = (z == 0) | (z == nz - 1)

    @pl.when(at_end)
    def _():
        settle(slots(0, 0, nz + 1, full), g_send)

    @pl.when(jnp.logical_not(at_end))
    def _():
        settle(slots(0, 0, 2 * nz + 1, full), g_send)

    settle(slots(0, 0, 2 * nz, full), p_send)
    settle(av.at[pl.ds(0, ncol * nout - 1)], a_send)
    settle(early.at[pl.ds(1, nout - 1)], e_sem.at[0])
    settle(earlyz.at[pl.ds(1, nz - 1)], ez_sem.at[0])
    settle(late.at[pl.ds(1, group - 1)], l_sem.at[0])
    settle(others, o_sem.at[0])
    settle(rowbuf.at[pl.ds(1, ncol - 1)], r_sem.at[0])


def update_kernel(edges, grad_ref, byrow_ref, bycol_ref, nr_ref, nc_ref, out_hbm, row_hbm, col_hbm, out, row, col, sem):
    parts = len(edges) - 1
    row[...] = nr_ref[...].reshape(row.shape)
    col[...] = nc_ref[...].reshape(col.shape)
    copies = [
        pltpu.make_async_copy(row, row_hbm, sem.at[parts]),
        pltpu.make_async_copy(col, col_hbm, sem.at[parts + 1]),
    ]
    for c in copies:
        c.start()
    for k in range(parts):
        here = pl.ds(edges[k], edges[k + 1] - edges[k])
        out[here, :] = (grad_ref[here, :] * jnp.tile(byrow_ref[here, :], (1, out.shape[1] // 128)) * bycol_ref[...]).astype(out.dtype)
        copies.append(pltpu.make_async_copy(out.at[here], out_hbm.at[here], sem.at[k]))
        copies[-1].start()
    for c in copies:
        c.wait()


def body(nout, nz, ncol, activations, out_grads, row_moment, col_moment):
    rows, width = row_moment.shape[0], col_moment.shape[0]
    ta, tg = activations.shape[0], out_grads.shape[0]
    tokens = ta * ncol * nout
    decay = 1.0 - STEP ** (-0.8)
    f32, bf16 = jnp.float32, jnp.bfloat16
    vmem = pl.BlockSpec(memory_space=pltpu.VMEM)
    hbm = pl.BlockSpec(memory_space=pl.ANY)
    dma = pltpu.SemaphoreType.DMA
    fine, chain, _, _, subs = cuts(width)
    wide = fine[2][0] + fine[2][1]
    grad, new_row, by_row, new_col, by_col = pl.pallas_call(
        functools.partial(kernel, nout, nz, ncol, 1.0 / tokens**0.5, decay),
        out_shape=(
            pltpu.VMEM((rows, width), f32),
            pltpu.VMEM((1, rows), f32),
            pltpu.VMEM((rows, 128), f32),
            pltpu.VMEM((1, width), f32),
            pltpu.VMEM((1, width), f32),
        ),
        in_specs=[hbm] * 4,
        out_specs=(vmem,) * 5,
        scratch_shapes=[
            pltpu.VMEM((tokens, width), bf16),
            pltpu.VMEM((nout * ncol, rows, ta), bf16),
            pltpu.VMEM(activations.shape, bf16),
            pltpu.VMEM((nout, rows, ta), bf16),
            pltpu.VMEM((rows,), f32),
            pltpu.VMEM((width,), f32),
            pltpu.VMEM((rows, 128), f32),
            pltpu.VMEM((nout, 1, wide), f32),
            pltpu.VMEM((nz, 1, wide), f32),
            pltpu.VMEM((nout * nz, 1, width - wide + 128), f32),
            pltpu.VMEM(((ncol - 1) * nout * nz, 1, 128), f32),
            pltpu.VMEM((ncol, 1, rows), f32),
            dma((nz - 1, len(chain))),
            dma((nz,)),
            dma((sum(map(len, subs)),)),
            dma((len(chain),)),
            dma((len(fine),)),
            dma((nout - 1,)),
            dma(()),
            dma(()),
            dma(()),
            dma(()),
            dma((2,)),
            dma((2,)), dma((2,)), dma((2,)), dma((2,)), dma((2,)),
            pltpu.SemaphoreType.REGULAR,
        ],
        compiler_params=pltpu.CompilerParams(
            collective_id=0, has_side_effects=True, vmem_limit_bytes=44 * 1024 * 1024
        ),
    )(
        activations,
        out_grads,
        pltpu.with_memory_space_constraint(row_moment, pltpu.HBM),
        pltpu.with_memory_space_constraint(col_moment, pltpu.HBM),
    )
    edges = [0, 16, 64, *range(192, rows + 1, 128)] if rows % 64 == 0 else [0, rows]
    return pl.pallas_call(
        functools.partial(update_kernel, edges),
        out_shape=(
            jax.ShapeDtypeStruct((rows, width), bf16),
            jax.ShapeDtypeStruct((rows,), f32),
            jax.ShapeDtypeStruct((width,), f32),
        ),
        in_specs=[vmem] * 5,
        out_specs=(hbm,) * 3,
        scratch_shapes=[
            pltpu.VMEM((rows, width), bf16),
            pltpu.VMEM((rows,), f32),
            pltpu.VMEM((width,), f32),
            dma((len(edges) + 1,)),
        ],
        compiler_params=pltpu.CompilerParams(vmem_limit_bytes=24 * 1024 * 1024),
    )(grad, by_row, by_col, new_row, new_col)


def solution(mesh):
    nout, nz, ncol = mesh.shape["outer"], mesh.shape["row"], mesh.shape["col"]
    return jax.shard_map(
        functools.partial(body, nout, nz, ncol),
        mesh=mesh,
        in_specs=(
            P(("outer", "col"), "row"),
            P(("outer", "row"), "col"),
            P(("row", "outer")),
            P("col"),
        ),
        out_specs=(P(("row", "outer"), "col"), P(("row", "outer")), P("col")),
        check_vma=False,
    )
```

```python
import functools

import jax
import jax.numpy as jnp
from jax import lax
from jax.experimental import pallas as pl
from jax.experimental.pallas import tpu as pltpu
from jax.sharding import PartitionSpec as P

D = 9216
F = 8192
STEP = 2
MESH = pl.DeviceIdType.MESH


def cuts(width):
    unit = width // 128
    share, *edges = [unit * e // 32 * 128 for e in (7, 8, 16, 24, 28, 32)]
    fine = [(a, b - a) for a, b in zip([0] + edges[:-1], edges)]
    chain = [[0, 1], [2, 3, 4]]
    by_y = (0, share)
    start, size = fine[-1]
    head = max(size // 256, 1) * 128
    lasts = [(start, head), (start + head, size - head)] if size > head else [(start, size)]
    subs = [[cols] for cols in fine[:-1]] + [lasts]
    by_z = [[(share, edges[0] - share)]] + subs[1:]
    return fine, chain, by_y, by_z, subs


def each(first, last, f):
    if last - first <= 32:
        for k in range(first, last):
            f(k)
    else:
        pl.loop(first, last)(f)


def kernel(
    nout, nz, ncol, scale, decay,
    raw_ref, g_ref, rm_hbm, cm_hbm,
    acc, nr_ref, byrow_ref, nc_ref, bycol_ref,
    gs, av, raw, a_ref, rm_ref, cm_ref, rowp, early, earlyz, late, others, rowbuf,
    gz_recv, gy_recv, last_recv, op_recv, od_recv, a1_recv, a2_recv,
    g_send, p_send, a_send, loc_sem,
    e_sem, ez_sem, l_sem, o_sem, r_sem, ready,
):
    tg, width = g_ref.shape
    rows, ta = av.shape[1], av.shape[2]
    fine, chain, by_y, by_z, subs = cuts(width)
    last = len(fine) - 1
    wide = early.shape[2]
    o = lax.axis_index("outer")
    z = lax.axis_index("row")
    x = lax.axis_index("col")
    y, core = o // 2, o % 2
    oy = (1 - y) * 2 + core
    op = y * 2 + (1 - core)
    od = (1 - y) * 2 + (1 - core)
    mate = z + 1 - 2 * (z % 2)
    end = jnp.where(z < nz // 2, nz - 1, 0)
    up = {"row": jnp.minimum(z + 1, nz - 1)}
    down = {"row": jnp.maximum(z - 1, 0)}

    def remote(src, dst, s, r, dev):
        return pltpu.make_async_remote_copy(
            src_ref=src, dst_ref=dst, send_sem=s, recv_sem=r, device_id=dev, device_id_type=MESH
        )

    def settle(ref, sem):
        pltpu.make_async_copy(ref, ref, sem).wait()

    def slots(oo, zz, count, cols):
        start = pl.multiple_of((oo * nz + zz) * tg, tg)
        return gs.at[pl.ds(start, count * tg), pl.ds(*cols)]

    def place(oo, zz, cols):
        return slots(oo, zz, 1, cols)

    full = (0, width)
    local_g = pltpu.make_async_copy(g_ref, slots(o, z, 1, full), loc_sem.at[0])
    load_a = pltpu.make_async_copy(raw_ref, raw, loc_sem.at[1])
    local_g.start()
    load_a.start()
    load_rm = pltpu.make_async_copy(rm_hbm, rm_ref, loc_sem.at[0])
    load_cm = pltpu.make_async_copy(cm_hbm, cm_ref, loc_sem.at[1])
    barrier = pltpu.get_barrier_semaphore()
    for who in (oy, op):
        pl.semaphore_signal(barrier, inc=1, device_id={"outer": who}, device_id_type=MESH)

    @pl.when(z > 0)
    def _():
        pl.semaphore_signal(barrier, inc=1, device_id=down, device_id_type=MESH)

    @pl.when(z < nz - 1)
    def _():
        pl.semaphore_signal(barrier, inc=1, device_id=up, device_id_type=MESH)

    for d in range(1, ncol):
        pl.semaphore_signal(barrier, inc=1, device_id={"col": (x + d) % ncol}, device_id_type=MESH)
    ends = jnp.where(z > 0, 1, 0) + jnp.where(z < nz - 1, 1, 0)
    pl.semaphore_wait(barrier, ncol + 1 + ends)

    def merged(c):
        first, end = fine[chain[c][0]], fine[chain[c][-1]]
        return (first[0], end[0] + end[1] - first[0])

    def from_z(zz, c, at):
        return gz_recv.at[(zz - at - 1 + 2 * nz) % nz, c]

    def to_up(src, zz, c):
        return remote(src, place(o, zz, merged(c)), g_send, from_z(zz, c, z + 1), up)

    def to_down(src, zz, c):
        return remote(src, place(o, zz, merged(c)), g_send, from_z(zz, c, z - 1), down)

    def to_y(src, zz, cols, sem, got):
        return remote(src, place(o, zz, cols), sem, got, {"outer": oy})

    def near(src, zz, c):
        return remote(src, place(o, zz, merged(c)), p_send, op_recv.at[c], {"outer": op})

    def over(zz, cols, h):
        here = place(oy, zz, cols)
        return remote(here, here, p_send, od_recv.at[h], {"outer": op})

    local_g.wait()
    for c in range(len(chain)):
        own = place(o, z, merged(c))

        @pl.when(z < nz - 1)
        def _():
            to_up(own, z, c).start()

        @pl.when(z > 0)
        def _():
            to_down(own, z, c).start()

        if c == 0:
            to_y(place(o, z, full), z, full, g_send, gy_recv.at[z]).start()
        near(own, z, c).start()

    def a_got(source, target):
        return a1_recv.at[(target - source + nout) % nout - 1]

    def a_first(target):
        return remote(a_ref.at[target], av.at[o * ncol + x], a_send, a_got(o, target), {"outer": target})

    def a_second(oo, d, own=False):
        k = oo * ncol + x
        return remote(a_ref.at[o] if own else av.at[k], av.at[k], a_send, a2_recv, {"col": (x + d) % ncol})

    local_a = pltpu.make_async_copy(a_ref.at[o], av.at[o * ncol + x], loc_sem.at[1])
    load_a.wait()
    turned = jnp.transpose(raw[...])
    for k in range(nout):
        a_ref[k] = turned[k * rows : (k + 1) * rows]

    def pass_on(oo):
        k = oo * ncol + x
        remote(av.at[k], av.at[k], a_send, a_got(oo, o), {"outer": oy}).wait_recv()
        for d in range(1, ncol):
            a_second(oo, d).start()

    def landed(zz, cols, sem):
        here = place(oy, zz, cols)
        remote(here, here, g_send, sem, {"outer": oy}).wait_recv()

    def take_whole(zz):
        landed(zz, full, gy_recv.at[zz])
        for h in range(len(fine)):
            over(zz, fine[h], h).start()

    def take(h):
        for i, cols in enumerate(subs[h]):
            both = slots(oy, 0, 2, cols)
            remote(both, both, g_send, last_recv.at[h + i], {"outer": oy}).wait_recv()
            over(end, cols, h).start()
            over(mate, cols, h).start()

    def relay(zz, c, onward):
        here = place(o, zz, merged(c))
        remote(here, here, g_send, from_z(zz, c, z), up).wait_recv()
        onward(here)

        @pl.when((zz != mate) & (zz != end))
        def _():
            to_y(here, zz, merged(c), g_send, gy_recv.at[zz]).start()

        @pl.when(zz == end)
        def _():
            for j in chain[c]:
                for i, cols in enumerate(subs[j]):
                    to_y(place(o, zz, cols), zz, cols, g_send, last_recv.at[j + i]).start()

        if c == 0:
            @pl.when(zz == mate)
            def _():
                to_y(place(o, zz, by_y), zz, by_y, g_send, last_recv.at[0]).start()

        near(here, zz, c).start()

    def extra():
        for h in range(len(fine)):
            for i, cols in enumerate(by_z[h]):
                here = place(oy, z, cols)

                @pl.when(mate > z)
                def _():
                    remote(here, here, g_send, last_recv.at[h + i], up).start()

                @pl.when(mate < z)
                def _():
                    remote(here, here, g_send, last_recv.at[h + i], down).start()

    def dots(oo, cols):
        total = None
        for k in range(ncol):
            block = oo * ncol + k
            part = jnp.dot(
                av[block],
                gs[pl.ds(pl.multiple_of(block * ta, ta), ta), cols],
                preferred_element_type=jnp.float32,
            )
            total = part if total is None else total + part
        return total

    def tiles(cols, f):
        start, size = cols
        tile = 512 if size % 512 == 0 else size

        @pl.loop(0, size // tile)
        def _(j):
            f(pl.multiple_of(j * tile, 128), tile)

    def first_half(c):
        slots_here = slots(op, 0, nz, merged(c))
        remote(slots_here, slots_here, p_send, op_recv.at[c], {"outer": op}).wait_recv()
        base = merged(c)[0]

        def one(offset, tile):
            cols = pl.ds(pl.multiple_of(base + offset, 128), tile)
            acc[:, cols] = dots(o, cols) + dots(op, cols)

        tiles(merged(c), one)

    def whole_from(d):
        for zz in (z - d, z + d):
            @pl.when((zz >= 0) & (zz < nz) & (zz != mate) & (zz != end))
            def _():
                take_whole(zz)

    for s in range(1, nz):
        if s == nz - 1:
            local_a.wait()
            load_rm.start()
            load_cm.start()
            settle(av.at[pl.ds(0, (ncol - 1) * nout)], a2_recv)
        for c in range(len(chain)):
            @pl.when(z - s >= 0)
            def _():
                def onward(here):
                    @pl.when(z < nz - 1)
                    def _():
                        to_up(here, z - s, c).start()

                relay(z - s, c, onward)

            @pl.when(z + s < nz)
            def _():
                def onward(here):
                    @pl.when(z > 0)
                    def _():
                        to_down(here, z + s, c).start()

                relay(z + s, c, onward)

            if s == 1 and c == 0:
                a_first(op).start()
                a_first(oy).start()
                for d in range(1, ncol):
                    a_second(o, d, True).start()
                local_a.start()
                pass_on(op)
                a_first(od).start()
            if s == nz - 1:
                first_half(c)
                if c == len(chain) - 2:
                    for d in (nz - 2, nz - 1):
                        whole_from(d)

        if s == 1:
            take_whole(z)
        if s == min(2, nz - 1):
            for c in range(2):
                pass_on((1 - y) * 2 + c)
        if s == max(nz - 2, 1):
            extra()
        if 1 < s < nz - 1:
            whole_from(s - 1)

    rowp[...] = jnp.zeros_like(rowp)
    load_rm.wait()
    load_cm.wait()
    old = rm_ref[...].reshape(1, rows)
    old_share = jnp.broadcast_to(jnp.sum(old, axis=1, keepdims=True) * (decay / ncol / 128), (1, 128))

    def finish(h, split=False):
        begin, size = fine[h]
        sums, shift = (early, 0) if begin < wide else (late, wide)

        def od_wait():
            here = slots(od, 0, nz, fine[h])
            remote(here, here, p_send, od_recv.at[h], {"outer": op}).wait_recv()

        def one(offset, tile):
            cols = pl.ds(pl.multiple_of(begin + offset, 128), tile)
            there = pl.ds(pl.multiple_of(begin - shift + offset, 128), tile)
            grad = acc[:, cols] + (dots(od, cols) if split else dots(oy, cols) + dots(od, cols))
            acc[:, cols] = grad
            squares = grad * grad
            part = squares[:, :128]
            for i in range(1, tile // 128):
                part = part + squares[:, i * 128 : (i + 1) * 128]
            rowp[...] += part
            sums[0, :, there] = jnp.sum(squares, axis=0, keepdims=True)

        def ahead(offset, tile):
            cols = pl.ds(pl.multiple_of(begin + offset, 128), tile)
            acc[:, cols] = acc[:, cols] + dots(oy, cols)

        if split:
            tiles(fine[h], ahead)
        od_wait()
        tiles(fine[h], one)

    def e_first(d):
        return remote(early.at[0], early.at[nout - d], e_sem.at[0], e_sem.at[1], {"outer": (o + d) % nout})

    def e_second(d):
        return remote(earlyz.at[0], earlyz.at[nz - d], ez_sem.at[0], ez_sem.at[1], {"row": (z + d) % nz})

    @pl.when(core == 1)
    def _():
        take(0)

    for h in range(len(fine)):
        @pl.when(core == 0)
        def _():
            take(h)

        if h < last:
            @pl.when(core == 1)
            def _():
                take(h + 1)

        finish(h, h == last)
        if fine[h][0] + fine[h][1] == wide:
            for d in range(1, nout):
                e_first(d).start()
            for d in range(1, ncol):
                pl.semaphore_signal(ready, inc=1, device_id={"col": (x + d) % ncol}, device_id_type=MESH)

    weight = (1.0 - decay) * scale * scale
    group = nout * nz
    rest = width - wide

    def mirror(k):
        return ((nout - k // nz) % nout) * nz + (nz - k % nz) % nz

    def peer(k, c):
        return {"outer": (o + k // nz) % nout, "row": (z + k % nz) % nz, "col": (x + c) % ncol}

    def send_late(k):
        remote(late.at[0], late.at[mirror(k)], l_sem.at[0], l_sem.at[1], peer(k, 0)).start()

    late[0, :, pl.ds(rest, 128)] = jnp.sum(rowp[...], axis=0, keepdims=True) * (weight / F) + old_share
    pl.semaphore_wait(ready, ncol - 1)
    for d in range(1, ncol):
        def send_other(k):
            slot = (ncol - d - 1) * group + mirror(k)
            remote(late.at[0, :, pl.ds(rest, 128)], others.at[slot], o_sem.at[0], o_sem.at[1], peer(k, d)).start()

        each(0, group, send_other)
    each(1, group, send_late)
    rowbuf[0] = jnp.sum(jnp.transpose(rowp[...]), axis=0, keepdims=True)

    def r_first(d):
        return remote(rowbuf.at[0], rowbuf.at[ncol - d], r_sem.at[0], r_sem.at[1], {"col": (x + d) % ncol})

    for d in range(1, ncol):
        r_first(d).start()
    settle(early.at[pl.ds(1, nout - 1)], e_sem.at[1])
    earlyz[0] = jnp.sum(early[...], axis=0)
    for d in range(1, nz):
        e_second(d).start()
    settle(rowbuf.at[pl.ds(1, ncol - 1)], r_sem.at[1])
    row_sq = jnp.sum(rowbuf[...], axis=0)
    new_row = decay * old + weight * row_sq / F
    nr_ref[...] = new_row
    byrow_ref[...] = jnp.transpose(jnp.broadcast_to(lax.rsqrt(new_row) * scale, (128, rows)))
    settle(earlyz.at[pl.ds(1, nz - 1)], ez_sem.at[1])
    cm = cm_ref[...].reshape(1, width)
    new_early = decay * cm[:, :wide] + weight * jnp.sum(earlyz[...], axis=0) / D
    nc_ref[:, :wide] = new_early
    settle(late.at[pl.ds(1, group - 1)], l_sem.at[1])
    arrived = jnp.sum(late[...], axis=0)
    new_late = decay * cm[:, wide:] + weight * arrived[:, :rest] / D
    nc_ref[:, wide:] = new_late
    roots = [lax.rsqrt(new_early), lax.rsqrt(new_late)]
    settle(others, o_sem.at[1])
    total = jnp.sum(arrived[:, rest:] + jnp.sum(others[...], axis=0), axis=1, keepdims=True)
    root = lax.rsqrt(D / total)
    bycol_ref[:, :wide] = roots[0] * root
    bycol_ref[:, wide:] = roots[1] * root

    at_end = (z == 0) | (z == nz - 1)

    @pl.when(at_end)
    def _():
        settle(slots(0, 0, nz + 1, full), g_send)

    @pl.when(jnp.logical_not(at_end))
    def _():
        settle(slots(0, 0, 2 * nz + 1, full), g_send)

    settle(slots(0, 0, 2 * nz, full), p_send)
    settle(av.at[pl.ds(0, ncol * nout - 1)], a_send)
    settle(early.at[pl.ds(1, nout - 1)], e_sem.at[0])
    settle(earlyz.at[pl.ds(1, nz - 1)], ez_sem.at[0])
    settle(late.at[pl.ds(1, group - 1)], l_sem.at[0])
    settle(others, o_sem.at[0])
    settle(rowbuf.at[pl.ds(1, ncol - 1)], r_sem.at[0])


def update_kernel(edges, grad_ref, byrow_ref, bycol_ref, nr_ref, nc_ref, out_hbm, row_hbm, col_hbm, out, row, col, sem):
    parts = len(edges) - 1
    row[...] = nr_ref[...].reshape(row.shape)
    col[...] = nc_ref[...].reshape(col.shape)
    copies = [
        pltpu.make_async_copy(row, row_hbm, sem.at[parts]),
        pltpu.make_async_copy(col, col_hbm, sem.at[parts + 1]),
    ]
    for c in copies:
        c.start()
    for k in range(parts):
        here = pl.ds(edges[k], edges[k + 1] - edges[k])
        out[here, :] = (grad_ref[here, :] * jnp.tile(byrow_ref[here, :], (1, out.shape[1] // 128)) * bycol_ref[...]).astype(out.dtype)
        copies.append(pltpu.make_async_copy(out.at[here], out_hbm.at[here], sem.at[k]))
        copies[-1].start()
    for c in copies:
        c.wait()


def body(nout, nz, ncol, activations, out_grads, row_moment, col_moment):
    rows, width = row_moment.shape[0], col_moment.shape[0]
    ta, tg = activations.shape[0], out_grads.shape[0]
    tokens = ta * ncol * nout
    decay = 1.0 - STEP ** (-0.8)
    f32, bf16 = jnp.float32, jnp.bfloat16
    vmem = pl.BlockSpec(memory_space=pltpu.VMEM)
    hbm = pl.BlockSpec(memory_space=pl.ANY)
    dma = pltpu.SemaphoreType.DMA
    fine, chain, _, _, subs = cuts(width)
    wide = fine[2][0] + fine[2][1]
    grad, new_row, by_row, new_col, by_col = pl.pallas_call(
        functools.partial(kernel, nout, nz, ncol, 1.0 / tokens**0.5, decay),
        out_shape=(
            pltpu.VMEM((rows, width), f32),
            pltpu.VMEM((1, rows), f32),
            pltpu.VMEM((rows, 128), f32),
            pltpu.VMEM((1, width), f32),
            pltpu.VMEM((1, width), f32),
        ),
        in_specs=[hbm] * 4,
        out_specs=(vmem,) * 5,
        scratch_shapes=[
            pltpu.VMEM((tokens, width), bf16),
            pltpu.VMEM((nout * ncol, rows, ta), bf16),
            pltpu.VMEM(activations.shape, bf16),
            pltpu.VMEM((nout, rows, ta), bf16),
            pltpu.VMEM((rows,), f32),
            pltpu.VMEM((width,), f32),
            pltpu.VMEM((rows, 128), f32),
            pltpu.VMEM((nout, 1, wide), f32),
            pltpu.VMEM((nz, 1, wide), f32),
            pltpu.VMEM((nout * nz, 1, width - wide + 128), f32),
            pltpu.VMEM(((ncol - 1) * nout * nz, 1, 128), f32),
            pltpu.VMEM((ncol, 1, rows), f32),
            dma((nz - 1, len(chain))),
            dma((nz,)),
            dma((sum(map(len, subs)),)),
            dma((len(chain),)),
            dma((len(fine),)),
            dma((nout - 1,)),
            dma(()),
            dma(()),
            dma(()),
            dma(()),
            dma((2,)),
            dma((2,)), dma((2,)), dma((2,)), dma((2,)), dma((2,)),
            pltpu.SemaphoreType.REGULAR,
        ],
        compiler_params=pltpu.CompilerParams(
            collective_id=0, has_side_effects=True, vmem_limit_bytes=44 * 1024 * 1024
        ),
    )(
        activations,
        out_grads,
        pltpu.with_memory_space_constraint(row_moment, pltpu.HBM),
        pltpu.with_memory_space_constraint(col_moment, pltpu.HBM),
    )
    edges = [0, 16, 64, *range(192, rows + 1, 128)] if rows % 64 == 0 else [0, rows]
    return pl.pallas_call(
        functools.partial(update_kernel, edges),
        out_shape=(
            jax.ShapeDtypeStruct((rows, width), bf16),
            jax.ShapeDtypeStruct((rows,), f32),
            jax.ShapeDtypeStruct((width,), f32),
        ),
        in_specs=[vmem] * 5,
        out_specs=(hbm,) * 3,
        scratch_shapes=[
            pltpu.VMEM((rows, width), bf16),
            pltpu.VMEM((rows,), f32),
            pltpu.VMEM((width,), f32),
            dma((len(edges) + 1,)),
        ],
        compiler_params=pltpu.CompilerParams(vmem_limit_bytes=24 * 1024 * 1024),
    )(grad, by_row, by_col, new_row, new_col)


def solution(mesh):
    nout, nz, ncol = mesh.shape["outer"], mesh.shape["row"], mesh.shape["col"]
    return jax.shard_map(
        functools.partial(body, nout, nz, ncol),
        mesh=mesh,
        in_specs=(
            P(("outer", "col"), "row"),
            P(("outer", "row"), "col"),
            P(("row", "outer")),
            P("col"),
        ),
        out_specs=(P(("row", "outer"), "col"), P(("row", "outer")), P("col")),
        check_vma=False,
    )
```
